128 devices in a mesh: tok: 16 (over z, x), exp: 8 (over y, core).
Axes of the slice: x: 4, y: 4, z: 4, core: 2. Of those that a mesh axis runs over, the one named last changes fastest.
Arguments:
- tokens: bfloat16 [3072, 2048], P('tok'), may hold values from -6 to 6
- gain_attn: float32 [2048], replicated, may hold values from 0.5 to 1.5
- router_attn: bfloat16 [2048, 8], replicated, may hold values from -0.125 to 0.125
- kv_weight: bfloat16 [2048, 4096], P(None, 'exp')
- query_weight: bfloat16 [8, 2048, 2048], P('exp', None, 'tok')
- out_weight: bfloat16 [8, 2048, 2048], P('exp', 'tok'), may hold values from -0.125 to 0.125
- gain_mlp: float32 [2048], replicated, may hold values from 0.5 to 1.5
- router_mlp: bfloat16 [2048, 8], replicated, may hold values from -0.125 to 0.125
- gate_weight: bfloat16 [8, 2048, 5632], P('exp', None, 'tok'), may hold values from -0.125 to 0.125
- up_weight: bfloat16 [8, 2048, 5632], P('exp', None, 'tok'), may hold values from -0.125 to 0.125
- down_weight: bfloat16 [8, 5632, 2048], P('exp', 'tok'), may hold values from -0.078125 to 0.078125
- routes_attn: int32 [3072, 2], P('tok'), may hold values from 0 to 7, all different within a row; in each aligned block of 192 rows (0 to 191, 192 to 383, ...) at most 96 rows name the same one
- routes_mlp: int32 [3072, 2], P('tok'), may hold values from 0 to 7, all different within a row; in each aligned block of 192 rows (0 to 191, 192 to 383, ...) at most 96 rows name the same one
- lengths: int32 [3], replicated, may hold values from 256 to 1536, as said below
- page_table: int32 [3, 12, 2], replicated, may hold values from 0 to 15, as said below
Outputs:
- mixed: bfloat16 [3072, 2048], P('tok', 'exp')
- kv_pages: bfloat16 [32, 128, 4096], P('tok', None, 'exp')
The draws below stay inside these ranges and needn't reach their ends.
Inputs may be any that keep to these rules, and one draw needn't show every extreme that they name: `routes_attn`: in each device's block of 192 tokens no expert is named by more than 96 tokens, a bound that some block reaches of them. `routes_mlp`: in each device's block of 192 tokens no expert is named by more than 96 tokens, a bound that some block reaches of them. The lengths sum to 3072; one prompt has exactly 1536 tokens. `page_table`: entry [s, i] holds (owner along tok, slot) of page i of prompt s, its tokens i * 128 to (i + 1) * 128 - 1; existing pages have distinct (owner, slot) pairs; the pages touched by one device's block of 192 tokens have distinct owners, so one block sends at most one page's tokens to an owner; entries past a prompt's last page are 0.
All inputs are finite; a program needn't handle non-finite values.
Results may differ from the reference program's by a relative error of at most 0.015.
The reference program's roundings to bfloat16 on the way count: a program that leaves them out, or rounds other values in their place, can miss the bound.
Values may be sent and summed in bfloat16 or wider, within the bound.
A program may use at most 128 MiB of HBM per device.

```python
import math
import jax
import jax.numpy as jnp
import numpy as np
from jax import lax

D = 2048
H = 16
HD = 128
FF = 5632
NEXP = 8
TOK_DEV = 192
PAGE = 128
CAP = 96
TOKENS = 3072
SEGMENT_LONGEST = 1536
SEGS = 3
PPS = 12
SLOTS = 2
POOL = 32
N_TOK = 16


def prompt_lengths(key):
    base_key = jax.random.fold_in(key, 5101)
    pick_key, weight_key = jax.random.split(base_key)
    minimal_length = 2 * PAGE
    chosen = jax.random.randint(pick_key, (), 0, SEGS)
    spare_tokens = TOKENS - SEGMENT_LONGEST - (SEGS - 1) * minimal_length
    draw_values = jax.random.randint(weight_key, (SEGS,), 1, 33)
    remaining_prompts = jnp.arange(SEGS) != chosen
    shares = jnp.where(remaining_prompts, draw_values * draw_values * draw_values, 0)
    share_total = jnp.sum(shares)
    surplus_tokens = spare_tokens * shares // share_total
    remainder_count = spare_tokens - jnp.sum(surplus_tokens)
    sorted_position = jnp.cumsum(remaining_prompts.astype(jnp.int32)) - 1
    additional_token = (remaining_prompts & (sorted_position < remainder_count)).astype(jnp.int32)
    lengths = jnp.where(remaining_prompts, minimal_length + surplus_tokens + additional_token, SEGMENT_LONGEST)
    return lengths.astype(jnp.int32)


def draw_lengths(key, part):
    return prompt_lengths(key)


def draw_page_table(key, part):
    lengths = prompt_lengths(key)
    page_counts = (lengths + PAGE - 1) // PAGE
    first_page = jnp.cumsum(page_counts) - page_counts
    page_index = jnp.arange(PPS)
    number = first_page[:, None] + page_index[None, :]
    exists = page_index[None, :] < page_counts[:, None]
    owners = jax.random.permutation(jax.random.fold_in(key, 5202), N_TOK)
    offset = jax.random.randint(jax.random.fold_in(key, 5203), (), 0, N_TOK)
    owner_ids = jnp.take(owners, (number + offset) % N_TOK)
    slot_ids = number // N_TOK
    page_entries = jnp.stack([jnp.where(exists, owner_ids, 0), jnp.where(exists, slot_ids, 0)], axis=-1)
    return page_entries.astype(jnp.int32)


def draw_query_weight(key, part):
    normal_part = jax.random.normal(jax.random.fold_in(key, 5301), (NEXP, D, H, HD), jnp.float32) / jnp.sqrt(jnp.float32(D))
    return normal_part.reshape(NEXP, D, H * HD).astype(jnp.bfloat16)


def draw_kv_weight(key, part):
    normal_part = jax.random.normal(jax.random.fold_in(key, 5302), (D, H, 2, HD), jnp.float32) / jnp.sqrt(jnp.float32(D))
    return normal_part.reshape(D, H * 2 * HD).astype(jnp.bfloat16)


def levels(rng, extent, cuts, least, high):
    def one(dim, parts):
        heights = jax.random.uniform(jax.random.fold_in(jax.random.fold_in(rng, 6), dim), (parts,), jnp.float32, least / len(cuts), high / len(cuts))
        return jnp.repeat(jnp.exp(heights), extent[dim] // parts).reshape((-1,) + (1,) * (len(extent) - dim - 1))

    level = one(*cuts[0])
    for cut in cuts[1:]:
        level = level * one(*cut)
    return level


def shared_out(own_key, own, number, rows, number_of, top, most, lean):
    sequence = jax.random.permutation(own_key, number_of)
    packed, usual = load_shares(number_of, rows * top, most, lean, True), load_shares(number_of, rows * top, most, lean, False)
    places = jnp.arange(number_of)

    def named(sizes, offset_by):
        used = int((sizes > 0).sum())
        fixed = max(1, used // 4)
        passed = fixed + (places - fixed + offset_by * (used - fixed)) % max(1, number_of - fixed)
        return jnp.zeros((number_of,), jnp.int32).at[sequence[jnp.where(places < fixed, places, passed)]].set(jnp.asarray(sizes, jnp.int32))

    sizes = jnp.where(number % 4 == 0, named(packed, number // 4), named(usual, number - number // 4 - 1))
    mixed = jax.random.permutation(jax.random.fold_in(own, 3), number_of)
    source_of, taker = mixed[0:number_of // 2 * 2:2], mixed[1:number_of // 2 * 2:2]
    slack = jnp.minimum(sizes[source_of] - 1, most - sizes[taker]) // 2
    slack = jnp.where((source_of == sequence[0]) | (taker == sequence[0]) | (sizes[taker] == 0), 0, jnp.maximum(slack, 0))
    passed = jax.random.randint(jax.random.fold_in(own, 4), (number_of // 2,), 0, 1 << 20) % (slack + 1)
    sizes = sizes.at[source_of].add(-passed).at[taker].add(passed)
    labels = jnp.searchsorted(jnp.cumsum(sizes), jnp.arange(rows * top), side="right").astype(jnp.int32)
    listing = labels.reshape(top, rows).T
    listing = listing[jax.random.permutation(jax.random.fold_in(own, 1), rows)]
    offset_by = jax.random.randint(jax.random.fold_in(own, 2), (rows, 1), 0, top)
    return jnp.take_along_axis(listing, (jnp.arange(top)[None, :] + offset_by) % top, axis=1)


def load_shares(count, total, most, slope, full):
    portions = [(1 << 20) // math.isqrt(standing ** slope) + 1 for standing in range(1, count + 1)]
    largest = most if full else min(most, max(-(-total // count), total * portions[0] // sum(portions)))
    least = 1 if total - largest >= count - 1 else 0
    counts, surplus = [largest] + [least] * (count - 1), total - largest - least * (count - 1)
    while surplus > 0:
        free = [i for i in range(1, count) if counts[i] < largest] or [i for i in range(1, count) if counts[i] < most]
        mass, remaining = sum([portions[i] for i in free]), surplus
        for i in free:
            more = min(most - counts[i], max(1, remaining * portions[i] // mass), surplus)
            counts[i] = counts[i] + more
            surplus = surplus - more
    return np.array(counts)


def gaussian(key, shape, width, limit, cuts=(), kind=jnp.bfloat16):
    loudness = levels(key, shape, cuts, -0.22, 0.18) if cuts else 1.0
    array = jax.random.normal(key, shape, jnp.float32) * width * loudness
    return jnp.minimum(jnp.maximum(array, -limit), limit).astype(kind)


def setup_inputs(seed: int = 0) -> dict:
    splits = jax.random.split(jax.random.key(seed), 16)
    tokens = gaussian(splits[0], (TOKENS, D), 1.0, 6.0, ((0, 16),))
    gain_attn = jnp.clip(1.0 + 0.1 * jax.random.normal(splits[1], (D,), jnp.float32), 0.5, 1.5)
    router_attn = gaussian(splits[2], (D, NEXP), D ** -0.5, 0.125)
    kv_weight = draw_kv_weight(jax.random.fold_in(splits[15], 71), 0)
    query_weight = draw_query_weight(jax.random.fold_in(splits[15], 71), 0)
    out_weight = gaussian(splits[5], (NEXP, H * HD, D), (H * HD) ** -0.5, 0.125, ((0, 8), (1, 16)))
    gain_mlp = jnp.clip(1.0 + 0.1 * jax.random.normal(splits[6], (D,), jnp.float32), 0.5, 1.5)
    router_mlp = gaussian(splits[7], (D, NEXP), D ** -0.5, 0.125)
    gate_weight = gaussian(splits[8], (NEXP, D, FF), D ** -0.5, 0.125, ((0, 8), (2, 16)))
    up_weight = gaussian(splits[9], (NEXP, D, FF), D ** -0.5, 0.125, ((0, 8), (2, 16)))
    down_weight = gaussian(splits[10], (NEXP, FF, D), FF ** -0.5, 0.078125, ((0, 8), (1, 16)))
    routes_attn_keys = jax.random.split(jax.random.fold_in(splits[11], 1), TOKENS // TOK_DEV)
    routes_attn_turns = jax.random.permutation(jax.random.fold_in(splits[11], 3), TOKENS // TOK_DEV)
    routes_attn = jax.vmap(lambda own, number: shared_out(jax.random.fold_in(splits[11], 2), own, number, TOK_DEV, NEXP, 2, CAP, 2))(routes_attn_keys, routes_attn_turns).reshape((TOKENS, 2))
    routes_mlp_keys = jax.random.split(jax.random.fold_in(splits[12], 1), TOKENS // TOK_DEV)
    routes_mlp_turns = jax.random.permutation(jax.random.fold_in(splits[12], 3), TOKENS // TOK_DEV)
    routes_mlp = jax.vmap(lambda own, number: shared_out(jax.random.fold_in(splits[12], 2), own, number, TOK_DEV, NEXP, 2, CAP, 1))(routes_mlp_keys, routes_mlp_turns).reshape((TOKENS, 2))
    lengths = draw_lengths(jax.random.fold_in(splits[15], 71), 0)
    page_table = draw_page_table(jax.random.fold_in(splits[15], 71), 0)
    return {"tokens": tokens, "gain_attn": gain_attn, "router_attn": router_attn, "kv_weight": kv_weight, "query_weight": query_weight, "out_weight": out_weight, "gain_mlp": gain_mlp, "router_mlp": router_mlp, "gate_weight": gate_weight, "up_weight": up_weight, "down_weight": down_weight, "routes_attn": routes_attn, "routes_mlp": routes_mlp, "lengths": lengths, "page_table": page_table}


epsilon = 1e-06

def normalize(values, gain):
    return values * lax.rsqrt(lax.optimization_barrier(jnp.mean(values * values, axis=-1, keepdims=True)) + epsilon) * gain

def rotate(values, position):
    half_width = values.shape[-1] // 2
    exponent = jnp.arange(half_width, dtype=jnp.float32) * (2.0 / values.shape[-1])
    frequency = jnp.power(jnp.float32(10000.0), -exponent)
    angles = position.astype(jnp.float32)[:, None] * frequency[None, :]
    cosine = jnp.cos(angles)[:, None, :]
    sine_part = jnp.sin(angles)[:, None, :]
    leading = values[..., :half_width]
    trailing = values[..., half_width:]
    return jnp.concatenate([leading * cosine - trailing * sine_part, trailing * cosine + leading * sine_part], axis=-1)

def locate(lengths, number):
    segment_ends = jnp.cumsum(lengths).astype(jnp.int32)
    segment_starts = (segment_ends - lengths).astype(jnp.int32)
    segment = lax.optimization_barrier(jnp.sum((number[:, None] >= segment_ends[None, :]).astype(jnp.int32), axis=1)).astype(jnp.int32)
    matched = segment[:, None] == jnp.arange(lengths.shape[0], dtype=jnp.int32)[None, :]
    start_of = lax.optimization_barrier(jnp.sum(jnp.where(matched, segment_starts[None, :], 0), axis=1)).astype(jnp.int32)
    return (segment, (number - start_of).astype(jnp.int32), start_of)

def pair_gates(logits, routes):
    leading = jnp.take_along_axis(logits, routes[:, 0:1], axis=1)[:, 0]
    trailing = jnp.take_along_axis(logits, routes[:, 1:2], axis=1)[:, 0]
    return (jax.nn.sigmoid(leading - trailing), jax.nn.sigmoid(trailing - leading))

def expert_gate(routes, leading, trailing, expert):
    return jnp.where(routes[:, 0] == expert, leading, 0.0) + jnp.where(routes[:, 1] == expert, trailing, 0.0)

def routed(routes, expert, capacity):
    chosen = (routes[:, 0] == expert) | (routes[:, 1] == expert)
    ranking = (jnp.cumsum(chosen.astype(jnp.int32)) - 1).astype(jnp.int32)
    target = jnp.where(chosen, ranking, capacity).astype(jnp.int32)
    picked = jnp.zeros((capacity,), jnp.int32).at[target].set(jnp.arange(routes.shape[0], dtype=jnp.int32), mode='drop')
    filled = jnp.arange(capacity, dtype=jnp.int32) < jnp.sum(chosen.astype(jnp.int32))
    return (picked, filled)

def attend_all(queries, key_heads, value_heads, picked, segment):
    query_segment = jnp.take(segment, picked)
    allowed = (segment[None, :] == query_segment[:, None]) & (jnp.arange(key_heads.shape[0], dtype=jnp.int32)[None, :] <= picked[:, None])
    score_scale = HD ** (-0.5)

    def one_head(operands):
        query_head, key_head, value_head = operands
        scores = jnp.dot(query_head, key_head.T, preferred_element_type=jnp.float32) * score_scale
        scores = jnp.where(allowed, scores, -jnp.inf)
        highest = lax.optimization_barrier(jnp.max(scores, axis=1, keepdims=True))
        weights = jnp.exp(scores - highest)
        denominator = lax.optimization_barrier(jnp.sum(weights, axis=1, keepdims=True))
        mixed_head = jnp.dot(weights.astype(jnp.bfloat16), value_head, preferred_element_type=jnp.float32) / denominator
        return mixed_head.astype(jnp.bfloat16)
    result = lax.map(one_head, (jnp.swapaxes(queries, 0, 1), jnp.swapaxes(key_heads, 0, 1), jnp.swapaxes(value_heads, 0, 1)))
    return jnp.swapaxes(result, 0, 1)

def reference(tokens, gain_attn, router_attn, kv_weight, query_weight, out_weight, gain_mlp, router_mlp, gate_weight, up_weight, down_weight, routes_attn, routes_mlp, lengths, page_table):
    widened = tokens.astype(jnp.float32)
    normed = normalize(widened, gain_attn).astype(jnp.bfloat16)
    number = jnp.arange(TOKENS, dtype=jnp.int32)
    segment, offset, start_of = locate(lengths, number)
    projected_kv = jnp.dot(normed, kv_weight, preferred_element_type=jnp.float32).reshape(TOKENS, H, 2, HD)
    key_heads = rotate(projected_kv[:, :, 0], offset).astype(jnp.bfloat16)
    value_heads = projected_kv[:, :, 1].astype(jnp.bfloat16)
    paired = jnp.stack([key_heads, value_heads], axis=2).reshape(TOKENS, H * 2 * HD)
    entries = jnp.take(page_table.reshape(-1, 2), segment * PPS + offset // PAGE, axis=0)
    location = ((entries[:, 0] * SLOTS + entries[:, 1]) * PAGE + offset % PAGE).astype(jnp.int32)
    kv_pages = jnp.zeros((POOL * PAGE, H * 2 * HD), jnp.bfloat16).at[location].set(paired).reshape(POOL, PAGE, H * 2 * HD)
    leading, trailing = pair_gates(jnp.dot(normed, router_attn, preferred_element_type=jnp.float32), routes_attn)
    capacity = N_TOK * CAP
    attn_out = jnp.zeros((TOKENS, D), jnp.float32)
    for expert in range(NEXP):
        picked, filled = routed(routes_attn, expert, capacity)
        expert_weight = expert_gate(routes_attn, leading, trailing, expert)
        chosen_rows = jnp.take(normed, picked, axis=0)
        projected_query = jnp.dot(chosen_rows, query_weight[expert], preferred_element_type=jnp.float32).reshape(capacity, H, HD)
        queries = rotate(projected_query, jnp.take(offset, picked)).astype(jnp.bfloat16)
        attended = attend_all(queries, key_heads, value_heads, picked, segment)
        projected = jnp.dot(attended.reshape(capacity, H * HD), out_weight[expert], preferred_element_type=jnp.float32)
        contribution = jnp.where(filled[:, None], projected * jnp.take(expert_weight, picked)[:, None], 0.0)
        attn_out = attn_out.at[picked].add(contribution)
    residual = widened + attn_out
    normed_mlp = normalize(residual, gain_mlp).astype(jnp.bfloat16)
    leading_mlp, trailing_mlp = pair_gates(jnp.dot(normed_mlp, router_mlp, preferred_element_type=jnp.float32), routes_mlp)
    slice_width = FF // N_TOK
    expert_sum = jnp.zeros((TOKENS, D), jnp.float32)
    for expert in range(NEXP):
        picked, filled = routed(routes_mlp, expert, capacity)
        expert_weight = expert_gate(routes_mlp, leading_mlp, trailing_mlp, expert)
        chosen_rows = jnp.take(normed_mlp, picked, axis=0)
        gate_part = jnp.dot(chosen_rows, gate_weight[expert], preferred_element_type=jnp.float32)
        upward = jnp.dot(chosen_rows, up_weight[expert], preferred_element_type=jnp.float32)
        hidden = (jax.nn.silu(gate_part) * upward).astype(jnp.bfloat16)
        pieces = jnp.einsum('cnf,nfd->ncd', hidden.reshape(capacity, N_TOK, slice_width).astype(jnp.float32), down_weight[expert].reshape(N_TOK, slice_width, D).astype(jnp.float32))
        rounded = lax.optimization_barrier(pieces.astype(jnp.bfloat16)).astype(jnp.float32)
        down_sum = lax.optimization_barrier(jnp.sum(rounded, axis=0))
        contribution = jnp.where(filled[:, None], down_sum * jnp.take(expert_weight, picked)[:, None], 0.0)
        expert_sum = expert_sum.at[picked].add(contribution)
    mixed = (residual + expert_sum).astype(jnp.bfloat16)
    return (mixed, kv_pages)
```

```python
import jax
import jax.numpy as jnp
from jax import lax
from jax.experimental import pallas as pl
from jax.experimental.pallas import tpu as pltpu
from jax.sharding import PartitionSpec as P

HD = 128
PAGE = 128
TOK_DEV = 192
TOKENS = 3072
D = 2048
FF_DEV = 352
HALF = 1024
QUARTER = 512
BLK = 384
SLOTS_BLK = 192
epsilon = 1e-06
MESH = pl.DeviceIdType.MESH
ANY = pl.BlockSpec(memory_space=pl.ANY)
VMEM = pl.BlockSpec(memory_space=pltpu.VMEM)
DIMS = ("z", "x", "y")
GATHER_ORDERS = (("z", "y", "x"), ("x", "z", "y"), ("y", "x", "z"))
SUM_ORDERS = (("x", "y", "z"), ("y", "z", "x"), ("z", "x", "y"))


class Place:
    def __init__(self):
        self.t = lax.axis_index("tok")
        self.e = lax.axis_index("exp")
        self.at = {"z": self.t // 4, "x": self.t % 4, "y": self.e // 2}
        self.c = self.e % 2

    def device(self, **moved):
        at = {**self.at, "c": self.c, **moved}
        return {"tok": at["z"] * 4 + at["x"], "exp": at["y"] * 2 + at["c"]}

    def step(self, dim, delta):
        return (self.at[dim] + delta) % 4

    def sibling(self):
        return self.device(c=1 - self.c)

    def neighbours(self):
        found = [self.sibling()]
        for dim in DIMS:
            found.append(self.device(**{dim: self.step(dim, 1)}))
            found.append(self.device(**{dim: self.step(dim, 3)}))
        return found


class Copies:
    def __init__(self, send, recv):
        self.send, self.recv, self.count, self.started = send, recv, 0, []

    def start(self, src, dst, device):
        number = self.count
        self.count += 1
        copy = pltpu.make_async_remote_copy(
            src_ref=src,
            dst_ref=dst,
            send_sem=self.send.at[number],
            recv_sem=self.recv.at[number],
            device_id=device,
            device_id_type=MESH,
        )
        copy.start()
        self.started.append(copy)
        return copy

    def drain(self):
        for copy in self.started:
            copy.wait_send()


def greet(partners):
    barrier = pltpu.get_barrier_semaphore()
    for partner in partners:
        pl.semaphore_signal(barrier, inc=1, device_id=partner, device_id_type=MESH)
    pl.semaphore_wait(barrier, len(partners))


def torus_gather(place, copies, out):
    c = place.c
    full = pl.ds(pl.multiple_of(c * HALF, HALF), HALF)
    first = pl.ds(pl.multiple_of(c * HALF, QUARTER), QUARTER)
    second = pl.ds(pl.multiple_of(c * HALF + QUARTER, QUARTER), QUARTER)
    sibling = place.sibling()
    handed = []

    def part(colour, stage, at, features):
        order = GATHER_ORDERS[colour]
        where = []
        for dim in DIMS:
            if dim in order[:stage]:
                where.append(slice(None))
            elif dim == order[stage]:
                where.append(at)
            else:
                where.append(place.at[dim])
        return out.at[(*where, colour, slice(None), features)]

    def send(colour, stage, at, features, device):
        region = part(colour, stage, at, features)
        return copies.start(region, region, device)

    def open_stage(colour, stage):
        dim = GATHER_ORDERS[colour][stage]
        right = place.device(**{dim: place.step(dim, 1)})
        left = place.device(**{dim: place.step(dim, 3)})
        own = place.at[dim]
        pair = (send(colour, stage, own, full, right), send(colour, stage, own, full, left))
        if stage == 2:
            handed.append(send(colour, stage, own, full, sibling))
        return (right, left, *pair)

    opened = [open_stage(colour, 0) for colour in range(3)]
    for stage in range(3):
        forwards = []
        for colour in range(3):
            dim = GATHER_ORDERS[colour][stage]
            right, left, to_right, to_left = opened[colour]
            to_right.wait_recv()
            on_right = send(colour, stage, place.step(dim, 3), first, right)
            if stage == 2:
                handed.append(send(colour, stage, place.step(dim, 3), full, sibling))
            to_left.wait_recv()
            on_left = send(colour, stage, place.step(dim, 1), second, left)
            if stage == 2:
                handed.append(send(colour, stage, place.step(dim, 1), full, sibling))
            forwards.append((on_right, on_left))
        for colour in range(3):
            dim = GATHER_ORDERS[colour][stage]
            on_right, on_left = forwards[colour]
            on_right.wait_recv()
            on_left.wait_recv()
            if stage < 2:
                opened[colour] = open_stage(colour, stage + 1)
            else:
                handed.append(send(colour, stage, place.step(dim, 2), full, sibling))
    for copy in handed:
        copy.wait_recv()


GATHER_COPIES = 3 * (3 * 4 + 4)


def sum_buffers(rows, width):
    shapes = []
    for lead in ((4, 4), (4,), ()):
        for size in (width // 2, width // 2, width, width):
            shapes.append(pltpu.VMEM((3, *lead, rows, size), jnp.bfloat16))
    return shapes


SUM_COPIES = 3 * 3 * 6


def torus_sum(place, copies, held, buffers):
    width = held.shape[-1]
    first, second, full = pl.ds(0, width // 2), pl.ds(width // 2, width // 2), slice(None)
    finals = []

    def part(colour, stage, at, features, inner=None):
        order = SUM_ORDERS[colour]
        where, inner = [], list(inner) if inner is not None else None
        for dim in DIMS:
            if dim in order[:stage]:
                where.append(place.at[dim])
            elif dim == order[stage]:
                where.append(at)
            else:
                where.append(slice(None) if inner is None else inner.pop(0))
        return held.at[(*where, colour, slice(None), features)]

    def each(stage, body):
        if stage == 0:

            def wide(number, carry):
                body((number // 4, number % 4))
                return carry

            lax.fori_loop(0, 16, wide, 0)
        elif stage == 1:
            for number in range(4):
                body((number,))
        else:
            body(())

    def add(colour, stage, at, features, arrived):
        def one(inner):
            target = part(colour, stage, at, features, inner)
            total = target[...].astype(jnp.float32)
            for ref in arrived:
                total = total + ref.at[(colour, *inner)][...].astype(jnp.float32)
            target[...] = total.astype(jnp.bfloat16)

        each(stage, one)

    def open_stage(colour, stage):
        dim = SUM_ORDERS[colour][stage]
        from_left, from_right, last_left, last_right = buffers[4 * stage : 4 * stage + 4]
        right = place.device(**{dim: place.step(dim, 1)})
        left = place.device(**{dim: place.step(dim, 3)})
        far, after, before = place.step(dim, 2), place.step(dim, 1), place.step(dim, 3)

        def lot(ref, features):
            return ref.at[colour] if features is None else ref.at[(colour, Ellipsis, features)]

        far_right = copies.start(part(colour, stage, far, first), lot(from_left, None), right)
        far_left = copies.start(part(colour, stage, far, second), lot(from_right, None), left)
        raw_right = copies.start(part(colour, stage, after, second), lot(last_left, second), right)
        raw_left = copies.start(part(colour, stage, before, first), lot(last_right, first), left)
        return (right, left, far_right, far_left, raw_right, raw_left)

    opened = [open_stage(colour, 0) for colour in range(3)]
    for stage in range(3):
        from_left, from_right, last_left, last_right = buffers[4 * stage : 4 * stage + 4]
        closing = []
        for colour in range(3):
            dim = SUM_ORDERS[colour][stage]
            right, left, far_right, far_left, raw_right, raw_left = opened[colour]
            after, before = place.step(dim, 1), place.step(dim, 3)
            far_right.wait_recv()
            add(colour, stage, after, first, (from_left,))
            sum_right = copies.start(
                part(colour, stage, after, first), last_left.at[(colour, Ellipsis, first)], right
            )
            far_left.wait_recv()
            add(colour, stage, before, second, (from_right,))
            sum_left = copies.start(
                part(colour, stage, before, second), last_right.at[(colour, Ellipsis, second)], left
            )
            closing.append((sum_right, sum_left))
        for colour in range(3):
            dim = SUM_ORDERS[colour][stage]
            raw_right, raw_left = opened[colour][4:]
            for copy in (raw_right, raw_left, *closing[colour]):
                copy.wait_recv()
            if stage < 2:
                add(colour, stage, place.at[dim], full, (last_left, last_right))
                opened[colour] = open_stage(colour, stage + 1)
            else:
                own = part(colour, stage, place.at[dim], full)[...].astype(jnp.float32)
                finals.append(
                    own
                    + last_left.at[colour][...].astype(jnp.float32)
                    + last_right.at[colour][...].astype(jnp.float32)
                )
    return finals


def spread_kernel(
    tokens_ref, gain_ref, kv_ref, routes_ref, wo_ref, wd_ref,
    out, wkv_out, routes_out, wo_out, wd_out,
    rows, send, recv, local,
):
    place = Place()
    copies = Copies(send, recv)
    t, e, c, y = place.t, place.e, place.c, place.at["y"]
    others = [{"tok": (t + delta) % 16, "exp": e} for delta in range(1, 16)]
    across = [{"tok": t, "exp": (e + delta) % 8} for delta in range(1, 8)]
    values = tokens_ref[y].astype(jnp.float32)
    scale = lax.rsqrt(jnp.mean(values * values, axis=-1, keepdims=True) + epsilon)
    rows[...] = (values * scale * gain_ref[...]).astype(jnp.bfloat16)
    half = pl.ds(pl.multiple_of(c * HALF, HALF), HALF)
    own = pltpu.make_async_copy(
        rows.at[:, :, half],
        out.at[place.at["z"], place.at["x"], y, :, :, half],
        local.at[0],
    )
    own.start()
    own_routes = pltpu.make_async_copy(routes_ref, routes_out.at[t], local.at[1])
    own_routes.start()
    greet(others + across)
    own.wait()
    side = Copies(send.at[pl.ds(GATHER_COPIES, 40)], recv.at[pl.ds(GATHER_COPIES, 40)])
    sibling = place.sibling()
    source = t // 2
    columns = pl.ds(pl.multiple_of((t % 2) * 256, 256), 256)
    mine = pl.ds(pl.multiple_of(c * HALF, HALF), HALF)
    theirs = pl.ds(pl.multiple_of((1 - c) * HALF, HALF), HALF)
    fan_send = [send.at[GATHER_COPIES + 40 + number] for number in range(7)]
    fan_recv = recv.at[GATHER_COPIES + 40]

    def fan(number, lines, device):
        return pltpu.make_async_remote_copy(
            src_ref=kv_ref.at[lines, columns],
            dst_ref=wkv_out.at[lines, :],
            send_sem=fan_send[number],
            recv_sem=fan_recv,
            device_id=device,
            device_id_type=MESH,
        )

    def fans():
        made = [fan(0, theirs, sibling)]
        for delta in range(1, 4):
            for core in range(2):
                made.append(
                    fan(
                        len(made),
                        pl.ds(core * HALF, HALF),
                        place.device(y=(y + delta) % 4, c=core),
                    )
                )
        return made

    @pl.when(e == source)
    def _():
        for copy in fans():
            copy.start()
        keep = pltpu.make_async_copy(kv_ref.at[mine, columns], wkv_out.at[mine, :], local.at[2])
        keep.start()
        keep.wait()

    routed = [
        side.start(routes_ref, routes_out.at[t], device) for device in others
    ]
    given_wo = side.start(wo_ref.at[:, theirs], wo_out, sibling)
    given_wd = []
    for number in range(4):
        lanes = pl.ds(pl.multiple_of(number * 512 + (1 - c) * 256, 256), 256)
        given_wd.append(side.start(wd_ref.at[:, lanes], wd_out.at[:, pl.ds(number * 256, 256)], sibling))
    torus_gather(place, copies, out)

    @pl.when(e != source)
    def _():
        fan(0, mine, sibling).wait_recv()

    shared = side.start(wkv_out.at[mine, :], wkv_out.at[mine, :], sibling)

    shared.wait_recv()
    own_routes.wait()
    for copy in routed + [given_wo] + given_wd:
        copy.wait_recv()

    @pl.when(e == source)
    def _():
        for copy in fans():
            copy.wait_send()

    copies.drain()
    side.drain()


def attend_kernel(
    scalars, x_ref, wqr_ref, wkv_ref, cos_ref, sin_ref, aux_ref, out_ref, keys, values
):
    block = pl.program_id(0)
    expert = scalars[8]
    rows = x_ref[...]
    query_part = jnp.dot(rows, wqr_ref[...], preferred_element_type=jnp.float32)
    kv_part = jnp.dot(rows, wkv_ref[...], preferred_element_type=jnp.float32)
    cosine, sine = cos_ref[...], sin_ref[...]

    def rotate(v):
        return (v * cosine + pltpu.roll(v, 64, 1) * sine).astype(jnp.bfloat16)

    here = pl.ds(pl.multiple_of(block * BLK, BLK), BLK)
    keys[here, :] = rotate(kv_part[:, :HD])
    values[here, :] = kv_part[:, HD:].astype(jnp.bfloat16)
    queries = rotate(query_part[:, :HD])
    logits = query_part[:, HD:]
    first, second, start = aux_ref[:, 0:1], aux_ref[:, 1:2], aux_ref[:, 4:5]
    chosen = (first == expert) | (second == expert)
    other = first + second - expert
    lane = lax.broadcasted_iota(jnp.int32, (BLK, HD), 1)
    own_logit = jnp.sum(jnp.where(lane == expert, logits, 0.0), axis=1, keepdims=True)
    other_logit = jnp.sum(jnp.where(lane == other, logits, 0.0), axis=1, keepdims=True)
    gate = jnp.where(chosen, 1.0 / (1.0 + jnp.exp(other_logit - own_logit)), 0.0)
    row_number = lax.broadcasted_iota(jnp.int32, (BLK, BLK), 0)
    column_number = lax.broadcasted_iota(jnp.int32, (BLK, BLK), 1)
    below = jnp.where(row_number >= column_number, 1.0, 0.0).astype(jnp.bfloat16)
    flags = jnp.broadcast_to(jnp.where(chosen, 1.0, 0.0), (BLK, HD)).astype(jnp.bfloat16)
    rank = jnp.dot(below, flags, preferred_element_type=jnp.float32)[:, 0:1] - 1.0
    slot = lax.broadcasted_iota(jnp.int32, (BLK, SLOTS_BLK), 1).astype(jnp.float32)
    placing = jnp.where(chosen & (rank == slot), 1.0, 0.0).astype(jnp.bfloat16)
    inside = lax.broadcasted_iota(jnp.int32, (BLK, HD), 0)
    digits = jnp.where(
        lane == 0,
        inside // 16,
        jnp.where(lane == 1, inside % 16, jnp.where(lane == 2, start // 64, jnp.where(lane == 3, start % 64, 0))),
    ).astype(jnp.float32).astype(jnp.bfloat16)
    across = (((0,), (0,)), ((), ()))
    picked = lax.dot_general(placing, queries, across, preferred_element_type=jnp.float32).astype(jnp.bfloat16)
    told = lax.dot_general(placing, digits, across, preferred_element_type=jnp.float32)
    highest_key = told[:, 0:1] * 16.0 + told[:, 1:2] + (block * BLK).astype(jnp.float32)
    lowest_key = told[:, 2:3] * 64.0 + told[:, 3:4]
    key_lane = lax.broadcasted_iota(jnp.int32, (SLOTS_BLK, BLK), 1)

    def visit(tile, carry):
        highest, denominator, summed = carry
        there = pl.ds(pl.multiple_of(tile * BLK, BLK), BLK)
        scores = lax.dot_general(
            picked, keys[there, :], (((1,), (1,)), ((), ())), preferred_element_type=jnp.float32
        ) * (HD**-0.5)
        number = (key_lane + tile * BLK).astype(jnp.float32)
        scores = jnp.where((number >= lowest_key) & (number <= highest_key), scores, -1e30)
        newest = jnp.maximum(highest, jnp.max(scores, axis=1, keepdims=True))
        weights = jnp.exp(scores - newest)
        shrink = jnp.exp(highest - newest)
        denominator = denominator * shrink + jnp.sum(weights, axis=1, keepdims=True)
        summed = summed * shrink + jnp.dot(
            weights.astype(jnp.bfloat16), values[there, :], preferred_element_type=jnp.float32
        )
        return newest, denominator, summed

    _, denominator, summed = lax.fori_loop(
        scalars[block],
        block + 1,
        visit,
        (
            jnp.full((SLOTS_BLK, 1), -1e30, jnp.float32),
            jnp.zeros((SLOTS_BLK, 1), jnp.float32),
            jnp.zeros((SLOTS_BLK, HD), jnp.float32),
        ),
    )
    attended = (summed / denominator).astype(jnp.bfloat16)
    dense = jnp.dot(placing, attended, preferred_element_type=jnp.float32)
    out_ref[...] = (dense * gate).astype(jnp.bfloat16)


def middle_kernel(
    heads_ref, wo_ref, wo_pair_ref, tokens_ref, gain_ref,
    out, residual_out,
    paired, weights, held, shared, squares, rows, residual, send, recv, local, *buffers,
):
    place = Place()
    t, e, c, y = place.t, place.e, place.c, place.at["y"]
    across = [{"tok": t, "exp": (e + delta) % 8} for delta in range(1, 8)]
    around = [device for number, device in enumerate(place.neighbours()) if number in (1, 2, 3, 4)]
    greet(around + across)
    copies = Copies(send, recv)
    sibling = place.sibling()
    half = pl.ds(pl.multiple_of(c * HALF, HALF), HALF)
    given = copies.start(heads_ref, paired, sibling)
    weights[0:HD, :] = wo_ref[:, half]
    weights[HD : 2 * HD, :] = wo_pair_ref[...]
    given.wait_recv()

    def project(number, carry):
        lines = pl.ds(pl.multiple_of(number * TOK_DEV, TOK_DEV), TOK_DEV)
        both = jnp.concatenate([heads_ref[lines, :], paired[lines, :]], axis=1)
        part = jnp.dot(both, weights[...], preferred_element_type=jnp.float32)
        held[number // 4, number % 4] = part.astype(jnp.bfloat16).reshape(4, 3, 16, HALF)
        return carry

    lax.fori_loop(0, 16, project, 0)
    sums = torus_sum(place, copies, held, buffers)
    square = []
    for colour in range(3):
        value = tokens_ref[y, colour, :, half].astype(jnp.float32) + sums[colour]
        residual[colour] = value
        square.append(jnp.sum(value * value, axis=-1, keepdims=True))
        shared[colour] = jnp.broadcast_to(square[colour], (16, HD))
    swapped = copies.start(shared, squares, sibling)
    for colour in range(3):
        for number in range(4):
            rows_here = pl.ds(colour * 16, 16)
            residual_out_part = residual[colour, :, number * 256 : (number + 1) * 256]
            buffers[-1][number, rows_here, :] = residual_out_part
    pieces = buffers[-1]
    base = send.shape[0] - 4

    def piece(number, sender):
        return pltpu.make_async_remote_copy(
            src_ref=pieces.at[number],
            dst_ref=residual_out.at[sender],
            send_sem=send.at[base + number],
            recv_sem=recv.at[base + sender],
            device_id={"tok": t, "exp": 4 * c + number},
            device_id_type=MESH,
        )

    for number in range(4):

        @pl.when(4 * c + number == e)
        def _():
            keep = pltpu.make_async_copy(pieces.at[number], residual_out.at[y], local.at[1])
            keep.start()
            keep.wait()

        @pl.when(4 * c + number != e)
        def _():
            piece(number, y).start()

    swapped.wait_recv()
    for colour in range(3):
        total = square[colour] + squares[colour][:, 0:1]
        scale = lax.rsqrt(total * (1.0 / D) + epsilon)
        rows[colour] = (residual[colour] * scale * gain_ref[:, half]).astype(jnp.bfloat16)
    own = pltpu.make_async_copy(
        rows, out.at[place.at["z"], place.at["x"], y, :, :, half], local.at[0]
    )
    own.start()
    own.wait()
    torus_gather(place, copies, out)
    for sender in range(4):
        itself = (y == sender) & (c == e // 4)

        @pl.when(jnp.logical_not(itself))
        def _():
            piece(0, sender).wait_recv()

    for number in range(4):

        @pl.when(4 * c + number != e)
        def _():
            piece(number, y).wait_send()

    copies.drain()


def hidden_kernel(scalars, x_ref, wg_ref, wu_ref, router_ref, aux_ref, out_ref):
    expert = scalars[8]
    rows = x_ref[...]
    logits = jnp.dot(rows, router_ref[...], preferred_element_type=jnp.float32)
    first, second = aux_ref[:, 2:3], aux_ref[:, 3:4]
    chosen = (first == expert) | (second == expert)
    other = first + second - expert
    lane = lax.broadcasted_iota(jnp.int32, (BLK, HD), 1)
    own_logit = jnp.sum(jnp.where(lane == expert, logits, 0.0), axis=1, keepdims=True)
    other_logit = jnp.sum(jnp.where(lane == other, logits, 0.0), axis=1, keepdims=True)
    gate = jnp.where(chosen, 1.0 / (1.0 + jnp.exp(other_logit - own_logit)), 0.0)
    opened = jnp.dot(rows, wg_ref[...], preferred_element_type=jnp.float32)
    upward = jnp.dot(rows, wu_ref[...], preferred_element_type=jnp.float32)
    hidden = opened / (1.0 + jnp.exp(-opened)) * upward
    out_ref[...] = (hidden * gate).astype(jnp.bfloat16)


def last_kernel(
    hidden_ref, wd_ref, wd_pair_ref, residual_ref,
    out_ref,
    paired, held, send, recv, *buffers,
):
    place = Place()
    c = place.c
    greet(place.neighbours())
    copies = Copies(send, recv)
    given = copies.start(hidden_ref, paired, place.sibling())
    given.wait_recv()

    def project(number, carry):
        lines = pl.ds(pl.multiple_of(number * TOK_DEV, TOK_DEV), TOK_DEV)
        own, pair = hidden_ref[lines, :], paired[lines, :]
        for at in range(4):
            lanes = pl.ds(pl.multiple_of(at * 512 + c * 256, 256), 256)
            part = jnp.dot(own, wd_ref[:, lanes], preferred_element_type=jnp.float32)
            part += jnp.dot(
                pair, wd_pair_ref[:, at * 256 : (at + 1) * 256], preferred_element_type=jnp.float32
            )
            held[number // 4, number % 4, at] = part.astype(jnp.bfloat16).reshape(3, 64, 256)
        return carry

    lax.fori_loop(0, 16, project, 0)
    sums = torus_sum(place, copies, held, buffers)
    for colour in range(3):
        lines = slice(colour * 64, (colour + 1) * 64)
        out_ref[lines, :] = (residual_ref[lines, :] + sums[colour]).astype(jnp.bfloat16)
    copies.drain()


def shards(
    tokens,
    gain_attn,
    router_attn,
    kv_weight,
    query_weight,
    out_weight,
    gain_mlp,
    router_mlp,
    gate_weight,
    up_weight,
    down_weight,
    routes_attn,
    routes_mlp,
    lengths,
    page_table,
):
    t = lax.axis_index("tok")
    e = lax.axis_index("exp")
    bf16 = jnp.bfloat16
    struct = jax.ShapeDtypeStruct
    tokens_parts = tokens.reshape(4, 3, 16, D)
    own_routes = jnp.concatenate([routes_attn, routes_mlp], axis=1).T
    own_routes = jnp.pad(own_routes, ((0, 4), (0, 64)))
    spread_count = GATHER_COPIES + 40 + 8
    gathered, wkv, routes, wo_pair, wd_pair = pl.pallas_call(
        spread_kernel,
        out_shape=(
            struct((4, 4, 4, 3, 16, D), bf16),
            struct((D, 256), bf16),
            struct((16, 8, 256), jnp.int32),
            struct((HD, HALF), bf16),
            struct((FF_DEV, HALF), bf16),
        ),
        in_specs=[VMEM, VMEM, ANY, ANY, ANY, ANY],
        out_specs=(ANY,) * 5,
        scratch_shapes=[
            pltpu.VMEM((3, 16, D), bf16),
            pltpu.SemaphoreType.DMA((spread_count,)),
            pltpu.SemaphoreType.DMA((spread_count,)),
            pltpu.SemaphoreType.DMA((3,)),
        ],
        compiler_params=pltpu.CompilerParams(collective_id=0, has_side_effects=True),
        name="spread",
    )(tokens_parts, gain_attn.reshape(1, 1, D), kv_weight, own_routes, out_weight[0], down_weight[0])
    h1 = gathered.reshape(TOKENS, D)

    ends = jnp.cumsum(lengths)
    starts = ends - lengths
    number = jnp.arange(TOKENS, dtype=jnp.int32)
    start_of = jnp.zeros((TOKENS,), jnp.int32)
    for prompt in range(1, lengths.shape[0]):
        start_of = jnp.where(number >= starts[prompt], starts[prompt], start_of)
    exponent = jnp.arange(64, dtype=jnp.float32) * (2.0 / HD)
    frequency = jnp.power(jnp.float32(10000.0), -exponent)
    angles = (number - start_of).astype(jnp.float32)[:, None] * frequency[None, :]
    cosine, sine = jnp.cos(angles), jnp.sin(angles)
    cos_table = jnp.concatenate([cosine, cosine], axis=1)
    sin_table = jnp.concatenate([-sine, sine], axis=1)
    aux = jnp.concatenate(
        [
            jnp.swapaxes(routes[:, :4, :TOK_DEV], 1, 2).reshape(TOKENS, 4),
            start_of[:, None],
            jnp.zeros((TOKENS, 3), jnp.int32),
        ],
        axis=1,
    )
    scalars = jnp.concatenate([start_of[::BLK] // BLK, e.reshape(1), jnp.zeros((7,), jnp.int32)]).astype(jnp.int32)
    wqr = jnp.concatenate([query_weight[0], jnp.pad(router_attn, ((0, 0), (0, HD - 8)))], axis=1)
    steps = TOKENS // BLK

    def whole(shape):
        return pl.BlockSpec(shape, lambda i, s: (0,) * len(shape))

    def lines(width):
        return pl.BlockSpec((BLK, width), lambda i, s: (i, 0))

    heads = pl.pallas_call(
        attend_kernel,
        out_shape=struct((TOKENS, HD), bf16),
        grid_spec=pltpu.PrefetchScalarGridSpec(
            num_scalar_prefetch=1,
            grid=(steps,),
            in_specs=[lines(D), whole((D, 256)), whole((D, 256)), lines(HD), lines(HD), lines(8)],
            out_specs=lines(HD),
            scratch_shapes=[pltpu.VMEM((TOKENS, HD), bf16), pltpu.VMEM((TOKENS, HD), bf16)],
        ),
        name="attend",
    )(scalars, h1, wqr, wkv, cos_table, sin_table, aux)

    pages = jnp.arange(page_table.shape[1], dtype=jnp.int32)
    exists = (pages[None, :] * PAGE < lengths[:, None]) & (page_table[:, :, 0] == t)
    page_rows, page_offsets, page_valid = [], [], []
    within = jnp.arange(PAGE, dtype=jnp.int32)
    for slot in range(2):
        here = (exists & (page_table[:, :, 1] == slot)).astype(jnp.int32)
        first_offset = jnp.sum(here * pages[None, :] * PAGE)
        length = jnp.sum(here * lengths[:, None])
        begin = jnp.sum(here * starts[:, None])
        offset = first_offset + within
        page_offsets.append(offset)
        page_valid.append(offset < length)
        page_rows.append(jnp.clip(begin + offset, 0, TOKENS - 1))
    page_offset = jnp.concatenate(page_offsets)
    page_kv = jnp.dot(
        jnp.take(h1, jnp.concatenate(page_rows), axis=0, mode="clip"),
        kv_weight,
        preferred_element_type=jnp.float32,
    ).reshape(2 * PAGE, 2, 2, HD)
    page_angles = page_offset.astype(jnp.float32)[:, None] * frequency[None, :]
    page_cos, page_sin = jnp.cos(page_angles)[:, None, :], jnp.sin(page_angles)[:, None, :]
    low, high = page_kv[:, :, 0, :64], page_kv[:, :, 0, 64:]
    page_keys = jnp.concatenate([low * page_cos - high * page_sin, high * page_cos + low * page_sin], axis=-1)
    page_kv = jnp.stack([page_keys, page_kv[:, :, 1]], axis=2).reshape(2 * PAGE, 512)
    kv_pages = jnp.where(jnp.concatenate(page_valid)[:, None], page_kv, 0.0).astype(bf16).reshape(2, PAGE, 512)

    middle_count = 2 + SUM_COPIES + GATHER_COPIES + 4
    gathered, residual = pl.pallas_call(
        middle_kernel,
        out_shape=(struct((4, 4, 4, 3, 16, D), bf16), struct((4, 48, 256), jnp.float32)),
        in_specs=[VMEM] * 5,
        out_specs=(ANY, ANY),
        scratch_shapes=[
            pltpu.VMEM((TOKENS, HD), bf16),
            pltpu.VMEM((2 * HD, HALF), bf16),
            pltpu.VMEM((4, 4, 4, 3, 16, HALF), bf16),
            pltpu.VMEM((3, 16, HD), jnp.float32),
            pltpu.VMEM((3, 16, HD), jnp.float32),
            pltpu.VMEM((3, 16, HALF), bf16),
            pltpu.VMEM((3, 16, HALF), jnp.float32),
            pltpu.SemaphoreType.DMA((middle_count,)),
            pltpu.SemaphoreType.DMA((middle_count,)),
            pltpu.SemaphoreType.DMA((2,)),
            *sum_buffers(16, HALF),
            pltpu.VMEM((4, 48, 256), jnp.float32),
        ],
        compiler_params=pltpu.CompilerParams(collective_id=1, has_side_effects=True),
        name="middle",
    )(heads, out_weight[0], wo_pair, tokens_parts, gain_mlp.reshape(1, D))
    h2 = gathered.reshape(TOKENS, D)

    hidden = pl.pallas_call(
        hidden_kernel,
        out_shape=struct((TOKENS, FF_DEV), bf16),
        grid_spec=pltpu.PrefetchScalarGridSpec(
            num_scalar_prefetch=1,
            grid=(steps,),
            in_specs=[lines(D), whole((D, FF_DEV)), whole((D, FF_DEV)), whole((D, HD)), lines(8)],
            out_specs=lines(FF_DEV),
        ),
        name="hidden",
    )(scalars, h2, gate_weight[0], up_weight[0], jnp.pad(router_mlp, ((0, 0), (0, HD - 8))), aux)

    last_count = 1 + SUM_COPIES
    mixed = pl.pallas_call(
        last_kernel,
        out_shape=struct((TOK_DEV, 256), bf16),
        in_specs=[VMEM] * 4,
        out_specs=VMEM,
        scratch_shapes=[
            pltpu.VMEM((TOKENS, FF_DEV), bf16),
            pltpu.VMEM((4, 4, 4, 3, 64, 256), bf16),
            pltpu.SemaphoreType.DMA((last_count,)),
            pltpu.SemaphoreType.DMA((last_count,)),
            *sum_buffers(64, 256),
        ],
        compiler_params=pltpu.CompilerParams(collective_id=2, has_side_effects=True),
        name="last",
    )(hidden, down_weight[0], wd_pair, residual.reshape(TOK_DEV, 256))
    return (mixed, kv_pages)


def solution(mesh):
    return jax.shard_map(
        shards,
        mesh=mesh,
        in_specs=(
            P("tok", None),
            P(),
            P(),
            P(None, "exp"),
            P("exp", None, "tok"),
            P("exp", "tok", None),
            P(),
            P(),
            P("exp", None, "tok"),
            P("exp", None, "tok"),
            P("exp", "tok", None),
            P("tok", None),
            P("tok", None),
            P(),
            P(),
        ),
        out_specs=(P("tok", "exp"), P("tok", None, "exp")),
        check_vma=False,
    )
```

```python
import jax
import jax.numpy as jnp
import numpy as np
from jax import lax
from jax.experimental import pallas as pl
from jax.experimental.pallas import tpu as pltpu
from jax.sharding import PartitionSpec as P

HD = 128
PAGE = 128
TOK_DEV = 192
TOKENS = 3072
D = 2048
FF_DEV = 352
HALF = 1024
QUARTER = 512
BLK = 384
SLOTS_BLK = 192
epsilon = 1e-06
MESH = pl.DeviceIdType.MESH
ANY = pl.BlockSpec(memory_space=pl.ANY)
VMEM = pl.BlockSpec(memory_space=pltpu.VMEM)
DIMS = ("z", "x", "y")
GATHER_ORDERS = (("z", "y", "x"), ("x", "z", "y"), ("y", "x", "z"))
SUM_ORDERS = (("x", "y", "z"), ("y", "z", "x"), ("z", "x", "y"))


class Place:
    def __init__(self):
        self.t = lax.axis_index("tok")
        self.e = lax.axis_index("exp")
        self.at = {"z": self.t // 4, "x": self.t % 4, "y": self.e // 2}
        self.c = self.e % 2

    def device(self, **moved):
        at = {**self.at, "c": self.c, **moved}
        return {"tok": at["z"] * 4 + at["x"], "exp": at["y"] * 2 + at["c"]}

    def step(self, dim, delta):
        return (self.at[dim] + delta) % 4

    def sibling(self):
        return self.device(c=1 - self.c)

    def neighbours(self):
        found = [self.sibling()]
        for dim in DIMS:
            found.append(self.device(**{dim: self.step(dim, 1)}))
            found.append(self.device(**{dim: self.step(dim, 3)}))
        return found


class Copies:
    def __init__(self, send, recv):
        self.send, self.recv, self.count, self.started = send, recv, 0, []

    def start(self, src, dst, device):
        number = self.count
        self.count += 1
        copy = pltpu.make_async_remote_copy(
            src_ref=src,
            dst_ref=dst,
            send_sem=self.send.at[number],
            recv_sem=self.recv.at[number],
            device_id=device,
            device_id_type=MESH,
        )
        copy.start()
        self.started.append(copy)
        return copy

    def drain(self):
        for copy in self.started:
            copy.wait_send()


def greet(partners):
    barrier = pltpu.get_barrier_semaphore()
    for partner in partners:
        pl.semaphore_signal(barrier, inc=1, device_id=partner, device_id_type=MESH)
    pl.semaphore_wait(barrier, len(partners))


def torus_gather(place, copies, out, hooks=()):
    c = place.c
    full = pl.ds(pl.multiple_of(c * HALF, HALF), HALF)
    first = pl.ds(pl.multiple_of(c * HALF, QUARTER), QUARTER)
    second = pl.ds(pl.multiple_of(c * HALF + QUARTER, QUARTER), QUARTER)
    sibling = place.sibling()
    handed = []
    colours = range(3)

    def hook(number):
        if number < len(hooks):
            hooks[number]()

    def send(colour, at, features, device):
        where = [at.get(dim, place.at[dim]) for dim in DIMS]
        region = out.at[(*where, colour, slice(None), features)]
        return copies.start(region, region, device)

    def pair(dim):
        return place.device(**{dim: place.step(dim, 1)}), place.device(**{dim: place.step(dim, 3)})

    def give(colour, at):
        handed.append(send(colour, at, full, sibling))

    everything = slice(None)
    begun = []
    for colour in colours:
        right, left = pair(GATHER_ORDERS[colour][0])
        begun.append((send(colour, {}, full, right), send(colour, {}, full, left)))
    hook(0)
    passed = []
    for colour in colours:
        dim = GATHER_ORDERS[colour][0]
        right, left = pair(dim)
        begun[colour][0].wait_recv()
        on_right = send(colour, {dim: place.step(dim, 3)}, first, right)
        begun[colour][1].wait_recv()
        on_left = send(colour, {dim: place.step(dim, 1)}, second, left)
        passed.append((on_right, on_left))

    groups = [{} for _ in colours]
    ahead = [{} for _ in colours]

    def place_of(colour, group, line):
        low, middle, high = GATHER_ORDERS[colour]
        return {low: everything, middle: place.step(middle, group), high: place.step(high, line)}

    def open_group(colour, group):
        right, left = pair(GATHER_ORDERS[colour][2])
        at = place_of(colour, group, 0)
        groups[colour][group] = (send(colour, at, full, right), send(colour, at, full, left))
        give(colour, at)

    def turn_group(colour, group):
        right, left = pair(GATHER_ORDERS[colour][2])
        to_right, to_left = groups[colour][group]
        to_right.wait_recv()
        on_right = send(colour, place_of(colour, group, 3), first, right)
        give(colour, place_of(colour, group, 3))
        to_left.wait_recv()
        on_left = send(colour, place_of(colour, group, 1), second, left)
        give(colour, place_of(colour, group, 1))
        ahead[colour][group] = (on_right, on_left)

    def close_group(colour, group):
        for copy in ahead[colour][group]:
            copy.wait_recv()
        give(colour, place_of(colour, group, 2))

    second_begun = []
    for colour in colours:
        for copy in passed[colour]:
            copy.wait_recv()
        low, middle, _ = GATHER_ORDERS[colour]
        right, left = pair(middle)
        at = {low: everything}
        second_begun.append(
            (
                send(colour, at, first, right),
                send(colour, at, second, left),
                send(colour, at, second, right),
                send(colour, at, first, left),
            )
        )
        open_group(colour, 0)
    hook(1)
    second_passed = []
    for colour in colours:
        low, middle, _ = GATHER_ORDERS[colour]
        right, left = pair(middle)
        near_right, near_left, rest_right, rest_left = second_begun[colour]
        near_right.wait_recv()
        on_right = send(colour, {low: everything, middle: place.step(middle, 3)}, first, right)
        near_left.wait_recv()
        on_left = send(colour, {low: everything, middle: place.step(middle, 1)}, second, left)
        second_passed.append((on_right, on_left))
    for colour in colours:
        second_begun[colour][2].wait_recv()
        open_group(colour, 3)
        second_begun[colour][3].wait_recv()
        open_group(colour, 1)
    for colour in colours:
        turn_group(colour, 0)
    hook(2)
    for colour in colours:
        for copy in second_passed[colour]:
            copy.wait_recv()
        open_group(colour, 2)
    for colour in colours:
        turn_group(colour, 3)
    for colour in colours:
        turn_group(colour, 1)
        close_group(colour, 0)
    hook(3)
    for colour in colours:
        turn_group(colour, 2)
        close_group(colour, 3)
        close_group(colour, 1)
    for colour in colours:
        close_group(colour, 2)
    for copy in handed:
        copy.wait_recv()


GATHER_COPIES = 3 * (4 + 6 + 16 + 16)


def sum_buffers(rows, width):
    shapes = []
    for lead in ((4, 4), (4,), ()):
        for size in (width // 2, width // 2, width, width):
            shapes.append(pltpu.VMEM((3, *lead, rows, size), jnp.bfloat16))
    return shapes


SUM_COPIES = 3 * 36


def torus_sum(place, copies, held, buffers):
    width = held.shape[-1]
    first, second, full = pl.ds(0, width // 2), pl.ds(width // 2, width // 2), slice(None)
    colours = range(3)
    order_of_groups = (2, 1, 3, 0)

    def part(colour, at, features):
        where = [at[dim] if dim in at else place.at[dim] for dim in DIMS]
        return held.at[(*where, colour, slice(None), features)]

    def add(colour, at, spread_over, features, arrived):
        def one(at, pieces):
            target = part(colour, at, features)
            total = target[...].astype(jnp.float32)
            for piece in pieces:
                total = total + piece[...].astype(jnp.float32)
            target[...] = total.astype(jnp.bfloat16)

        if spread_over is None:
            one(at, arrived)
        else:

            def step(number, carry):
                one({**at, spread_over: number}, [piece.at[number] for piece in arrived])
                return carry

            lax.fori_loop(0, 4, step, 0)

    def lanes(ref, features):
        return ref if features is None else ref.at[(Ellipsis, features)]

    class Ring:
        def __init__(self, colour, dim, fixed, spread_over, refs):
            self.colour, self.dim, self.fixed, self.spread_over, self.refs = colour, dim, fixed, spread_over, refs
            self.right = place.device(**{dim: place.step(dim, 1)})
            self.left = place.device(**{dim: place.step(dim, 3)})

        def at(self, delta):
            return {**self.fixed, self.dim: place.step(self.dim, delta)}

        def send(self, delta, features, target, device):
            return copies.start(part(self.colour, self.at(delta), features), target, device)

        def far(self):
            self.far_right = self.send(2, first, self.refs[0], self.right)
            self.far_left = self.send(2, second, self.refs[1], self.left)

        def raw_right_part(self):
            self.raw_right = self.send(1, second, lanes(self.refs[2], second), self.right)

        def raw_left_part(self):
            self.raw_left = self.send(3, first, lanes(self.refs[3], first), self.left)

        def pass_right(self):
            self.far_right.wait_recv()
            add(self.colour, self.at(1), self.spread_over, first, [self.refs[0]])
            self.sum_right = self.send(1, first, lanes(self.refs[2], first), self.right)

        def pass_left(self):
            self.far_left.wait_recv()
            add(self.colour, self.at(3), self.spread_over, second, [self.refs[1]])
            self.sum_left = self.send(3, second, lanes(self.refs[3], second), self.left)

        def arrive(self):
            for copy in (self.raw_right, self.raw_left, self.sum_right, self.sum_left):
                copy.wait_recv()

        def close(self):
            self.arrive()
            add(self.colour, self.at(0), self.spread_over, full, [self.refs[2], self.refs[3]])

    rings, seconds, thirds = [], [], []
    for colour in colours:
        wide, middle, narrow = SUM_ORDERS[colour]
        by_group = []
        for number, group in enumerate(order_of_groups):
            refs = [ref.at[colour, number] for ref in buffers[0:4]]
            fixed = {middle: place.step(middle, group), narrow: slice(None)}
            by_group.append(Ring(colour, wide, fixed, narrow, refs))
        rings.append(by_group)
        refs = [ref.at[colour] for ref in buffers[4:8]]
        seconds.append(Ring(colour, middle, {narrow: slice(None)}, narrow, refs))
        thirds.append(Ring(colour, narrow, {}, None, [ref.at[colour] for ref in buffers[8:12]]))

    def open_ring(ring):
        ring.far()
        ring.raw_right_part()
        ring.raw_left_part()

    for number in range(2):
        for colour in colours:
            open_ring(rings[colour][number])
    for number in range(4):
        for colour in colours:
            rings[colour][number].pass_right()
            rings[colour][number].pass_left()
        if number + 2 < 4:
            for colour in colours:
                open_ring(rings[colour][number + 2])
        for colour in colours:
            rings[colour][number].close()
            if number == 0:
                seconds[colour].far()
            elif number == 1:
                seconds[colour].raw_right_part()
            elif number == 2:
                seconds[colour].raw_left_part()
                seconds[colour].pass_right()
                seconds[colour].pass_left()
    for colour in colours:
        seconds[colour].close()
        open_ring(thirds[colour])
    for colour in colours:
        thirds[colour].pass_right()
        thirds[colour].pass_left()
    finals = []
    for colour in colours:
        thirds[colour].arrive()
        own = part(colour, {}, full)[...].astype(jnp.float32)
        last_left, last_right = thirds[colour].refs[2:4]
        finals.append(own + last_left[...].astype(jnp.float32) + last_right[...].astype(jnp.float32))
    return finals


def spread_kernel(
    tokens_ref, gain_ref, kv_ref, routes_attn_ref, routes_mlp_ref, wo_ref, wd_ref,
    out, wkv_out, routes_out, wo_out, wd_out,
    rows, routes, send, recv, local,
):
    place = Place()
    copies = Copies(send, recv)
    t, e, c, y = place.t, place.e, place.c, place.at["y"]
    others = [{"tok": (t + delta) % 16, "exp": e} for delta in range(1, 16)]
    across = [{"tok": t, "exp": (e + delta) % 8} for delta in range(1, 8)]
    values = tokens_ref[y].astype(jnp.float32)
    scale = lax.rsqrt(jnp.mean(values * values, axis=-1, keepdims=True) + epsilon)
    rows[...] = (values * scale * gain_ref[...]).astype(jnp.bfloat16)
    half = pl.ds(pl.multiple_of(c * HALF, HALF), HALF)
    own = pltpu.make_async_copy(
        rows.at[:, :, half],
        out.at[place.at["z"], place.at["x"], y, :, :, half],
        local.at[0],
    )
    own.start()
    routes[...] = jnp.zeros_like(routes)
    routes[0:2, 0:TOK_DEV] = routes_attn_ref[...].astype(jnp.float32)
    routes[2:4, 0:TOK_DEV] = routes_mlp_ref[...].astype(jnp.float32)
    greet(others + across)
    own.wait()
    own_routes = pltpu.make_async_copy(routes, routes_out.at[t], local.at[1])
    own_routes.start()
    side = Copies(send.at[pl.ds(GATHER_COPIES, 24)], recv.at[pl.ds(GATHER_COPIES, 24)])
    sibling = place.sibling()
    source = t // 2
    hops = (y + 4 - t // 4) % 4
    columns = pl.ds(pl.multiple_of((t % 2) * 256, 256), 256)
    mine = pl.ds(pl.multiple_of(c * HALF, HALF), HALF)
    theirs = pl.ds(pl.multiple_of((1 - c) * HALF, HALF), HALF)
    rising = pl.ds(pl.multiple_of(c * HALF, QUARTER), QUARTER)
    falling = pl.ds(pl.multiple_of(c * HALF + QUARTER, QUARTER), QUARTER)
    right = place.device(y=(y + 1) % 4)
    left = place.device(y=(y + 3) % 4)
    is_source = e == source

    def fan(number, lines, device, fresh=False):
        at = GATHER_COPIES + 24 + number
        return pltpu.make_async_remote_copy(
            src_ref=kv_ref.at[lines, columns] if fresh else wkv_out.at[lines, :],
            dst_ref=wkv_out.at[lines, :],
            send_sem=send.at[at],
            recv_sem=recv.at[at],
            device_id=device,
            device_id_type=MESH,
        )

    keep = pltpu.make_async_copy(kv_ref.at[mine, columns], wkv_out.at[mine, :], local.at[2])

    def first_hop():
        @pl.when(is_source)
        def _():
            fan(0, theirs, sibling, True).start()
            fan(1, rising, right, True).start()
            fan(2, falling, left, True).start()
            keep.start()

        for device in others:
            routed.append(side.start(routes, routes_out.at[t], device))
        routed.append(side.start(wo_ref.at[:, theirs], wo_out, sibling))
        for number in range(4):
            lanes = pl.ds(pl.multiple_of(number * 512 + (1 - c) * 256, 256), 256)
            target = wd_out.at[:, pl.ds(number * 256, 256)]
            routed.append(side.start(wd_ref.at[:, lanes], target, sibling))

    def second_hop():
        @pl.when((hops == 0) & jnp.logical_not(is_source))
        def _():
            fan(0, mine, sibling).wait_recv()
            fan(1, rising, right).start()
            fan(2, falling, left).start()

        @pl.when(hops == 1)
        def _():
            fan(1, rising, right).wait_recv()
            fan(1, rising, right).start()

        @pl.when(hops == 3)
        def _():
            fan(2, falling, left).wait_recv()
            fan(2, falling, left).start()

    def third_hop():
        @pl.when(hops == 2)
        def _():
            fan(1, rising, right).wait_recv()
            fan(1, rising, right).start()
            fan(2, falling, left).wait_recv()
            fan(2, falling, left).start()

    def last_hop():
        @pl.when(hops == 1)
        def _():
            fan(2, falling, left).wait_recv()

        @pl.when(hops == 3)
        def _():
            fan(1, rising, right).wait_recv()

        @pl.when(is_source)
        def _():
            keep.wait()

        shared.append(side.start(wkv_out.at[mine, :], wkv_out.at[mine, :], sibling))

    routed, shared = [], []
    torus_gather(place, copies, out, (first_hop, second_hop, third_hop, last_hop))
    shared[0].wait_recv()
    own_routes.wait()
    for copy in routed:
        copy.wait_recv()

    @pl.when(is_source)
    def _():
        fan(0, theirs, sibling, True).wait_send()

    @pl.when(hops != 3)
    def _():
        fan(1, rising, right).wait_send()

    @pl.when(hops != 1)
    def _():
        fan(2, falling, left).wait_send()

    copies.drain()
    side.drain()


def route_columns(routes_ref):
    eye = jnp.where(
        lax.broadcasted_iota(jnp.int32, (8, HD), 0) == lax.broadcasted_iota(jnp.int32, (8, HD), 1), 1.0, 0.0
    )
    parts = [
        lax.dot_general(
            routes_ref[number][:, :TOK_DEV], eye, (((0,), (0,)), ((), ())), preferred_element_type=jnp.float32
        )
        for number in range(2)
    ]
    return jnp.concatenate(parts, axis=0)


def pair_gate(first, second, expert, logits, base):
    chosen = (first == expert) | (second == expert)
    other = first + second - expert
    lane = lax.broadcasted_iota(jnp.int32, logits.shape, 1).astype(jnp.float32) - base
    own_logit = jnp.sum(jnp.where(lane == expert, logits, 0.0), axis=1, keepdims=True)
    other_logit = jnp.sum(jnp.where(lane == other, logits, 0.0), axis=1, keepdims=True)
    return chosen, jnp.where(chosen, 1.0 / (1.0 + jnp.exp(other_logit - own_logit)), 0.0)


PAGE_ROWS = PAGE + 16


def attend_kernel(
    lengths, table, x_ref, h1_ref, wq_ref, wkv_ref, router_ref, kv_ref, frequency_ref, routes_ref,
    out_ref, pages_ref,
    keys, values, weights, inner_cos, inner_sin, page_rows, page_sems,
):
    block = pl.program_id(0)
    tok = lax.axis_index("tok")
    expert = lax.axis_index("exp").astype(jnp.float32)
    second_start = lengths[0]
    third_start = lengths[0] + lengths[1]
    frequency = jnp.broadcast_to(frequency_ref[...], (8, HD))
    sign = jnp.where(lax.broadcasted_iota(jnp.int32, (1, HD), 1) < 64, -1.0, 1.0)

    def find(slot):
        def look(number, carry):
            begin, count, start = carry
            prompt, page = number // table.shape[1], number % table.shape[1]
            its_start = jnp.where(prompt == 0, 0, jnp.where(prompt == 1, second_start, third_start))
            remaining = lengths[prompt] - page * PAGE
            hit = (table[prompt, page, 0] == tok) & (table[prompt, page, 1] == slot) & (remaining > 0)
            return (
                jnp.where(hit, its_start + page * PAGE, begin),
                jnp.where(hit, jnp.minimum(remaining, PAGE), count),
                jnp.where(hit, its_start, start),
            )

        zero = jnp.int32(0)
        begin, count, start = lax.fori_loop(0, table.shape[0] * table.shape[1], look, (zero, zero, zero))
        aligned = jnp.minimum(begin // 16 * 16, TOKENS - PAGE_ROWS)
        return begin, count, start, pl.multiple_of(aligned, 16)

    def page_copy(slot, aligned):
        return pltpu.make_async_copy(
            h1_ref.at[pl.ds(aligned, PAGE_ROWS), :], page_rows.at[slot], page_sems.at[slot]
        )

    @pl.when(block == 0)
    def _():
        for slot in range(2):
            page_copy(slot, find(slot)[3]).start()
        weights[:, 0:HD] = wq_ref[...]
        weights[:, HD : 3 * HD] = wkv_ref[...]
        eye = jnp.where(
            lax.broadcasted_iota(jnp.int32, (8, HD), 0) == lax.broadcasted_iota(jnp.int32, (8, HD), 1), 1.0, 0.0
        )
        weights[:, 3 * HD :] = lax.dot_general(
            router_ref[...].astype(jnp.float32), eye, (((0,), (0,)), ((), ())), preferred_element_type=jnp.float32
        ).astype(jnp.bfloat16)
        angle = lax.broadcasted_iota(jnp.int32, (BLK, HD), 0).astype(jnp.float32) * frequency_ref[...]
        inner_cos[...] = jnp.cos(angle)
        inner_sin[...] = jnp.sin(angle)

    def outer(offset):
        angle = frequency * offset.astype(jnp.float32)
        return jnp.cos(angle)[0:1], jnp.sin(angle)[0:1]

    def turn(base_cos, base_sin, in_cos, in_sin):
        return base_cos * in_cos - base_sin * in_sin, (base_sin * in_cos + base_cos * in_sin) * sign

    row = lax.broadcasted_iota(jnp.int32, (BLK, 1), 0) + block * BLK
    in_second, in_third = row >= second_start, row >= third_start
    start = jnp.where(in_third, third_start, jnp.where(in_second, second_start, 0))
    bases = [outer(block * BLK - begin) for begin in (jnp.int32(0), second_start, third_start)]
    base_cos, base_sin = (
        jnp.where(in_third, bases[2][number], jnp.where(in_second, bases[1][number], bases[0][number]))
        for number in range(2)
    )
    cosine, sine = turn(base_cos, base_sin, inner_cos[...], inner_sin[...])

    def rotate(v):
        return (v * cosine + pltpu.roll(v, 64, 1) * sine).astype(jnp.bfloat16)

    projected = jnp.dot(x_ref[...], weights[...], preferred_element_type=jnp.float32)
    here = pl.ds(pl.multiple_of(block * BLK, BLK), BLK)
    keys[here, :] = rotate(projected[:, HD : 2 * HD])
    values[here, :] = projected[:, 2 * HD : 3 * HD].astype(jnp.bfloat16)
    queries = rotate(projected[:, :HD])
    columns = route_columns(routes_ref)
    chosen, gate = pair_gate(columns[:, 0:1], columns[:, 1:2], expert, projected[:, 3 * HD :], 0.0)
    row_number = lax.broadcasted_iota(jnp.int32, (BLK, BLK), 0)
    column_number = lax.broadcasted_iota(jnp.int32, (BLK, BLK), 1)
    below = jnp.where(row_number >= column_number, 1.0, 0.0).astype(jnp.bfloat16)
    flags = jnp.broadcast_to(jnp.where(chosen, 1.0, 0.0), (BLK, HD)).astype(jnp.bfloat16)
    rank = jnp.dot(below, flags, preferred_element_type=jnp.float32)[:, 0:1] - 1.0
    slot_number = lax.broadcasted_iota(jnp.int32, (BLK, SLOTS_BLK), 1).astype(jnp.float32)
    placing = jnp.where(chosen & (rank == slot_number), 1.0, 0.0).astype(jnp.bfloat16)
    lane = lax.broadcasted_iota(jnp.int32, (BLK, HD), 1)
    inside = lax.broadcasted_iota(jnp.int32, (BLK, HD), 0)
    digits = jnp.where(
        lane == 0,
        inside // 16,
        jnp.where(lane == 1, inside % 16, jnp.where(lane == 2, start // 64, jnp.where(lane == 3, start % 64, 0))),
    ).astype(jnp.float32).astype(jnp.bfloat16)
    taken = lax.dot_general(
        placing,
        jnp.concatenate([queries, digits], axis=1),
        (((0,), (0,)), ((), ())),
        preferred_element_type=jnp.float32,
    )
    picked = taken[:, :HD].astype(jnp.bfloat16)
    told = taken[:, HD:]
    highest_key = told[:, 0:1] * 16.0 + told[:, 1:2] + (block * BLK).astype(jnp.float32)
    lowest_key = told[:, 2:3] * 64.0 + told[:, 3:4]
    key_lane = lax.broadcasted_iota(jnp.int32, (SLOTS_BLK, BLK), 1)

    def visit(tile, carry):
        highest, denominator, summed = carry
        there = pl.ds(pl.multiple_of(tile * BLK, BLK), BLK)
        scores = lax.dot_general(
            picked, keys[there, :], (((1,), (1,)), ((), ())), preferred_element_type=jnp.float32
        ) * (HD**-0.5)
        number = (key_lane + tile * BLK).astype(jnp.float32)
        scores = jnp.where((number >= lowest_key) & (number <= highest_key), scores, -1e30)
        newest = jnp.maximum(highest, jnp.max(scores, axis=1, keepdims=True))
        shares = jnp.exp(scores - newest)
        shrink = jnp.exp(highest - newest)
        denominator = denominator * shrink + jnp.sum(shares, axis=1, keepdims=True)
        summed = summed * shrink + jnp.dot(
            shares.astype(jnp.bfloat16), values[there, :], preferred_element_type=jnp.float32
        )
        return newest, denominator, summed

    begin = block * BLK
    begin_of = jnp.where(begin >= third_start, third_start, jnp.where(begin >= second_start, second_start, 0))
    _, denominator, summed = lax.fori_loop(
        begin_of // BLK,
        block + 1,
        visit,
        (
            jnp.full((SLOTS_BLK, 1), -1e30, jnp.float32),
            jnp.zeros((SLOTS_BLK, 1), jnp.float32),
            jnp.zeros((SLOTS_BLK, HD), jnp.float32),
        ),
    )
    attended = (summed / denominator).astype(jnp.bfloat16)
    dense = jnp.dot(placing, attended, preferred_element_type=jnp.float32)
    out_ref[...] = (dense * gate).astype(jnp.bfloat16)

    @pl.when(block == pl.num_programs(0) - 1)
    def _():
        for slot in range(2):
            begin, count, start, aligned = find(slot)
            page_copy(slot, aligned).wait()
            part = jnp.dot(page_rows[slot], kv_ref[...], preferred_element_type=jnp.float32)
            page_cos, page_sin = turn(*outer(aligned - start), inner_cos[0:PAGE_ROWS], inner_sin[0:PAGE_ROWS])
            pieces = []
            for head in range(2):
                key = part[:, head * 256 : head * 256 + HD]
                pieces.append(key * page_cos + pltpu.roll(key, 64, 1) * page_sin)
                pieces.append(part[:, head * 256 + HD : (head + 1) * 256])
            run = jnp.concatenate(pieces, axis=1).astype(jnp.bfloat16)
            to = lax.broadcasted_iota(jnp.int32, (PAGE, PAGE_ROWS), 0)
            source = lax.broadcasted_iota(jnp.int32, (PAGE, PAGE_ROWS), 1)
            moving = jnp.where((source == to + (begin - aligned)) & (to < count), 1.0, 0.0).astype(jnp.bfloat16)
            pages_ref[slot] = jnp.dot(moving, run, preferred_element_type=jnp.float32).astype(jnp.bfloat16)


def middle_kernel(
    heads_ref, wo_ref, wo_pair_ref, tokens_ref, gain_ref,
    out, residual_out,
    paired, weights, held, shared, squares, rows, residual, send, recv, local, *buffers,
):
    place = Place()
    t, e, c, y = place.t, place.e, place.c, place.at["y"]
    across = [{"tok": t, "exp": (e + delta) % 8} for delta in range(1, 8)]
    around = [device for number, device in enumerate(place.neighbours()) if number in (1, 2, 3, 4)]
    greet(around + across)
    copies = Copies(send, recv)
    sibling = place.sibling()
    half = pl.ds(pl.multiple_of(c * HALF, HALF), HALF)
    given = copies.start(heads_ref, paired, sibling)
    weights[0:HD, :] = wo_ref[:, half]
    weights[HD : 2 * HD, :] = wo_pair_ref[...]
    given.wait_recv()

    def project(number, carry):
        lines = pl.ds(pl.multiple_of(number * TOK_DEV, TOK_DEV), TOK_DEV)
        both = jnp.concatenate([heads_ref[lines, :], paired[lines, :]], axis=1)
        part = jnp.dot(both, weights[...], preferred_element_type=jnp.float32)
        held[number // 4, number % 4] = part.astype(jnp.bfloat16).reshape(4, 3, 16, HALF)
        return carry

    lax.fori_loop(0, 16, project, 0)
    sums = torus_sum(place, copies, held, buffers)
    square = []
    for colour in range(3):
        value = tokens_ref[y, colour, :, half].astype(jnp.float32) + sums[colour]
        residual[colour] = value
        square.append(jnp.sum(value * value, axis=-1, keepdims=True))
        shared[colour] = jnp.broadcast_to(square[colour], (16, HD))
    swapped = copies.start(shared, squares, sibling)
    for colour in range(3):
        for number in range(4):
            rows_here = pl.ds(colour * 16, 16)
            residual_out_part = residual[colour, :, number * 256 : (number + 1) * 256]
            buffers[-1][number, rows_here, :] = residual_out_part
    pieces = buffers[-1]
    base = send.shape[0] - 4

    def piece(number, sender):
        return pltpu.make_async_remote_copy(
            src_ref=pieces.at[number],
            dst_ref=residual_out.at[sender],
            send_sem=send.at[base + number],
            recv_sem=recv.at[base + sender],
            device_id={"tok": t, "exp": 4 * c + number},
            device_id_type=MESH,
        )

    for number in range(4):

        @pl.when(4 * c + number == e)
        def _():
            keep = pltpu.make_async_copy(pieces.at[number], residual_out.at[y], local.at[1])
            keep.start()
            keep.wait()

        @pl.when(4 * c + number != e)
        def _():
            piece(number, y).start()

    swapped.wait_recv()
    for colour in range(3):
        total = square[colour] + squares[colour][:, 0:1]
        scale = lax.rsqrt(total * (1.0 / D) + epsilon)
        rows[colour] = (residual[colour] * scale * gain_ref[:, half]).astype(jnp.bfloat16)
    own = pltpu.make_async_copy(
        rows, out.at[place.at["z"], place.at["x"], y, :, :, half], local.at[0]
    )
    own.start()
    own.wait()
    torus_gather(place, copies, out)
    for sender in range(4):
        itself = (y == sender) & (c == e // 4)

        @pl.when(jnp.logical_not(itself))
        def _():
            piece(0, sender).wait_recv()

    for number in range(4):

        @pl.when(4 * c + number != e)
        def _():
            piece(number, y).wait_send()

    copies.drain()


def hidden_kernel(x_ref, wg_ref, wu_ref, router_ref, routes_ref, out_ref, weights):
    expert = lax.axis_index("exp").astype(jnp.float32)

    @pl.when(pl.program_id(0) == 0)
    def _():
        weights[0:FF_DEV, :] = wg_ref[...]
        weights[FF_DEV:BLK, :] = jnp.zeros((BLK - FF_DEV, D), jnp.bfloat16)
        weights[BLK : BLK + FF_DEV, :] = wu_ref[...]
        weights[BLK + FF_DEV :, :] = jnp.zeros((BLK - FF_DEV, D), jnp.bfloat16)
        router = jnp.concatenate([router_ref[...].astype(jnp.float32), jnp.zeros((8, D), jnp.float32)], axis=0)
        weights[BLK + FF_DEV : BLK + FF_DEV + 16, :] = router.astype(jnp.bfloat16)

    both = lax.dot_general(
        x_ref[...], weights[...], (((1,), (1,)), ((), ())), preferred_element_type=jnp.float32
    )
    columns = route_columns(routes_ref)
    _, gate = pair_gate(columns[:, 2:3], columns[:, 3:4], expert, both[:, 5 * HD :], float(FF_DEV - 2 * HD))
    opened, upward = both[:, :FF_DEV], both[:, BLK : BLK + FF_DEV]
    hidden = opened / (1.0 + jnp.exp(-opened)) * upward
    out_ref[...] = (hidden * gate).astype(jnp.bfloat16)


def last_kernel(
    hidden_ref, wd_ref, wd_pair_ref, residual_ref,
    out_ref,
    paired, held, send, recv, *buffers,
):
    place = Place()
    c = place.c
    greet(place.neighbours())
    copies = Copies(send, recv)
    given = copies.start(hidden_ref, paired, place.sibling())
    given.wait_recv()

    def project(number, carry):
        lines = pl.ds(pl.multiple_of(number * TOK_DEV, TOK_DEV), TOK_DEV)
        own, pair = hidden_ref[lines, :], paired[lines, :]
        for at in range(4):
            lanes = pl.ds(pl.multiple_of(at * 512 + c * 256, 256), 256)
            part = jnp.dot(own, wd_ref[:, lanes], preferred_element_type=jnp.float32)
            part += jnp.dot(
                pair, wd_pair_ref[:, at * 256 : (at + 1) * 256], preferred_element_type=jnp.float32
            )
            held[number // 4, number % 4, at] = part.astype(jnp.bfloat16).reshape(3, 64, 256)
        return carry

    lax.fori_loop(0, 16, project, 0)
    sums = torus_sum(place, copies, held, buffers)
    for colour in range(3):
        lines = slice(colour * 64, (colour + 1) * 64)
        out_ref[lines, :] = (residual_ref[lines, :] + sums[colour]).astype(jnp.bfloat16)
    copies.drain()


def shards(
    tokens,
    gain_attn,
    router_attn,
    kv_weight,
    query_weight,
    out_weight,
    gain_mlp,
    router_mlp,
    gate_weight,
    up_weight,
    down_weight,
    routes_attn,
    routes_mlp,
    lengths,
    page_table,
):
    bf16 = jnp.bfloat16
    struct = jax.ShapeDtypeStruct
    tokens_parts = tokens.reshape(4, 3, 16, D)
    spread_count = GATHER_COPIES + 24 + 3
    gathered, wkv, routes, wo_pair, wd_pair = pl.pallas_call(
        spread_kernel,
        out_shape=(
            struct((4, 4, 4, 3, 16, D), bf16),
            struct((D, 256), bf16),
            struct((16, 8, 256), jnp.float32),
            struct((HD, HALF), bf16),
            struct((FF_DEV, HALF), bf16),
        ),
        in_specs=[VMEM, VMEM, ANY, VMEM, VMEM, ANY, ANY],
        out_specs=(ANY,) * 5,
        scratch_shapes=[
            pltpu.VMEM((3, 16, D), bf16),
            pltpu.VMEM((8, 256), jnp.float32),
            pltpu.SemaphoreType.DMA((spread_count,)),
            pltpu.SemaphoreType.DMA((spread_count,)),
            pltpu.SemaphoreType.DMA((3,)),
        ],
        compiler_params=pltpu.CompilerParams(collective_id=0, has_side_effects=True),
        name="spread",
    )(
        tokens_parts, gain_attn.reshape(1, 1, D), kv_weight, routes_attn.T, routes_mlp.T, out_weight[0], down_weight[0]
    )
    h1 = gathered.reshape(TOKENS, D)
    frequency = (10000.0 ** -(np.arange(HD) % 64 * (2.0 / HD))).astype(np.float32).reshape(1, HD)
    steps = TOKENS // BLK

    def whole(*shape):
        return pl.BlockSpec(shape, lambda i, *_: (0,) * len(shape))

    def lines(width):
        return pl.BlockSpec((BLK, width), lambda i, *_: (i, 0))

    routes_spec = pl.BlockSpec((2, 8, 256), lambda i, *_: (i, 0, 0))
    heads, kv_pages = pl.pallas_call(
        attend_kernel,
        out_shape=(struct((TOKENS, HD), bf16), struct((2, PAGE, 512), bf16)),
        grid_spec=pltpu.PrefetchScalarGridSpec(
            num_scalar_prefetch=2,
            grid=(steps,),
            in_specs=[
                lines(D), ANY, whole(D, HD), whole(D, 256), whole(8, D), whole(D, 512), whole(1, HD), routes_spec,
            ],
            out_specs=(lines(HD), whole(2, PAGE, 512)),
            scratch_shapes=[
                pltpu.VMEM((TOKENS, HD), bf16),
                pltpu.VMEM((TOKENS, HD), bf16),
                pltpu.VMEM((D, 4 * HD), bf16),
                pltpu.VMEM((BLK, HD), jnp.float32),
                pltpu.VMEM((BLK, HD), jnp.float32),
                pltpu.VMEM((2, PAGE_ROWS, D), bf16),
                pltpu.SemaphoreType.DMA((2,)),
            ],
        ),
        name="attend",
    )(lengths, page_table, h1, h1, query_weight[0], wkv, router_attn.T, kv_weight, jnp.asarray(frequency), routes)

    middle_count = 2 + SUM_COPIES + GATHER_COPIES + 4
    gathered, residual = pl.pallas_call(
        middle_kernel,
        out_shape=(struct((4, 4, 4, 3, 16, D), bf16), struct((4, 48, 256), jnp.float32)),
        in_specs=[VMEM] * 5,
        out_specs=(ANY, ANY),
        scratch_shapes=[
            pltpu.VMEM((TOKENS, HD), bf16),
            pltpu.VMEM((2 * HD, HALF), bf16),
            pltpu.VMEM((4, 4, 4, 3, 16, HALF), bf16),
            pltpu.VMEM((3, 16, HD), jnp.float32),
            pltpu.VMEM((3, 16, HD), jnp.float32),
            pltpu.VMEM((3, 16, HALF), bf16),
            pltpu.VMEM((3, 16, HALF), jnp.float32),
            pltpu.SemaphoreType.DMA((middle_count,)),
            pltpu.SemaphoreType.DMA((middle_count,)),
            pltpu.SemaphoreType.DMA((2,)),
            *sum_buffers(16, HALF),
            pltpu.VMEM((4, 48, 256), jnp.float32),
        ],
        compiler_params=pltpu.CompilerParams(collective_id=1, has_side_effects=True),
        name="middle",
    )(heads, out_weight[0], wo_pair, tokens_parts, gain_mlp.reshape(1, D))
    h2 = gathered.reshape(TOKENS, D)

    hidden = pl.pallas_call(
        hidden_kernel,
        out_shape=struct((TOKENS, FF_DEV), bf16),
        grid_spec=pltpu.PrefetchScalarGridSpec(
            num_scalar_prefetch=0,
            grid=(steps,),
            in_specs=[lines(D), whole(FF_DEV, D), whole(FF_DEV, D), whole(8, D), routes_spec],
            out_specs=lines(FF_DEV),
            scratch_shapes=[pltpu.VMEM((2 * BLK, D), bf16)],
        ),
        name="hidden",
    )(h2, gate_weight[0].T, up_weight[0].T, router_mlp.T, routes)

    last_count = 1 + SUM_COPIES
    mixed = pl.pallas_call(
        last_kernel,
        out_shape=struct((TOK_DEV, 256), bf16),
        in_specs=[VMEM] * 4,
        out_specs=VMEM,
        scratch_shapes=[
            pltpu.VMEM((TOKENS, FF_DEV), bf16),
            pltpu.VMEM((4, 4, 4, 3, 64, 256), bf16),
            pltpu.SemaphoreType.DMA((last_count,)),
            pltpu.SemaphoreType.DMA((last_count,)),
            *sum_buffers(64, 256),
        ],
        compiler_params=pltpu.CompilerParams(collective_id=2, has_side_effects=True),
        name="last",
    )(hidden, down_weight[0], wd_pair, residual.reshape(TOK_DEV, 256))
    return (mixed, kv_pages)


def solution(mesh):
    return jax.shard_map(
        shards,
        mesh=mesh,
        in_specs=(
            P("tok", None),
            P(),
            P(),
            P(None, "exp"),
            P("exp", None, "tok"),
            P("exp", "tok", None),
            P(),
            P(),
            P("exp", None, "tok"),
            P("exp", None, "tok"),
            P("exp", "tok", None),
            P("tok", None),
            P("tok", None),
            P(),
            P(),
        ),
        out_specs=(P("tok", "exp"), P("tok", None, "exp")),
        check_vma=False,
    )
```

```python
import jax
import jax.numpy as jnp
import numpy as np
from jax import lax
from jax.experimental import pallas as pl
from jax.experimental.pallas import tpu as pltpu
from jax.sharding import PartitionSpec as P

HD = 128
PAGE = 128
TOK_DEV = 192
TOKENS = 3072
D = 2048
FF_DEV = 352
HALF = 1024
QUARTER = 512
BLK = 384
SLOTS_BLK = 192
epsilon = 1e-06
MESH = pl.DeviceIdType.MESH
ANY = pl.BlockSpec(memory_space=pl.ANY)
VMEM = pl.BlockSpec(memory_space=pltpu.VMEM)
DIMS = ("z", "x", "y")
GATHER_ORDERS = (("z", "y", "x"), ("x", "z", "y"), ("y", "x", "z"))
SUM_ORDERS = (("x", "y", "z"), ("y", "z", "x"), ("z", "x", "y"))


class Place:
    def __init__(self):
        self.t = lax.axis_index("tok")
        self.e = lax.axis_index("exp")
        self.at = {"z": self.t // 4, "x": self.t % 4, "y": self.e // 2}
        self.c = self.e % 2

    def device(self, **moved):
        at = {**self.at, "c": self.c, **moved}
        return {"tok": at["z"] * 4 + at["x"], "exp": at["y"] * 2 + at["c"]}

    def step(self, dim, delta):
        return (self.at[dim] + delta) % 4

    def sibling(self):
        return self.device(c=1 - self.c)

    def neighbours(self):
        found = [self.sibling()]
        for dim in DIMS:
            found.append(self.device(**{dim: self.step(dim, 1)}))
            found.append(self.device(**{dim: self.step(dim, 3)}))
        return found


class Copies:
    def __init__(self, send, recv):
        self.send, self.recv, self.count, self.started = send, recv, 0, []

    def start(self, src, dst, device):
        number = self.count
        self.count += 1
        copy = pltpu.make_async_remote_copy(
            src_ref=src,
            dst_ref=dst,
            send_sem=self.send.at[number],
            recv_sem=self.recv.at[number],
            device_id=device,
            device_id_type=MESH,
        )
        copy.start()
        self.started.append(copy)
        return copy

    def drain(self):
        for copy in self.started:
            copy.wait_send()


def greet(partners):
    barrier = pltpu.get_barrier_semaphore()
    for partner in partners:
        pl.semaphore_signal(barrier, inc=1, device_id=partner, device_id_type=MESH)
    pl.semaphore_wait(barrier, len(partners))


def torus_gather(place, copies, out, hooks=()):
    c = place.c
    full = pl.ds(pl.multiple_of(c * HALF, HALF), HALF)
    first = pl.ds(pl.multiple_of(c * HALF, QUARTER), QUARTER)
    second = pl.ds(pl.multiple_of(c * HALF + QUARTER, QUARTER), QUARTER)
    sibling = place.sibling()
    handed = []
    colours = range(3)

    def hook(number):
        if number < len(hooks):
            hooks[number]()

    def send(colour, at, features, device):
        where = [at.get(dim, place.at[dim]) for dim in DIMS]
        region = out.at[(*where, colour, slice(None), features)]
        return copies.start(region, region, device)

    def pair(dim):
        return place.device(**{dim: place.step(dim, 1)}), place.device(**{dim: place.step(dim, 3)})

    def give(colour, at):
        handed.append(send(colour, at, full, sibling))

    everything = slice(None)
    begun = []
    for colour in colours:
        right, left = pair(GATHER_ORDERS[colour][0])
        begun.append((send(colour, {}, full, right), send(colour, {}, full, left)))
    hook(0)
    passed = []
    for colour in colours:
        dim = GATHER_ORDERS[colour][0]
        right, left = pair(dim)
        begun[colour][0].wait_recv()
        on_right = send(colour, {dim: place.step(dim, 3)}, first, right)
        begun[colour][1].wait_recv()
        on_left = send(colour, {dim: place.step(dim, 1)}, second, left)
        passed.append((on_right, on_left))

    groups = [{} for _ in colours]
    ahead = [{} for _ in colours]

    def place_of(colour, group, line):
        low, middle, high = GATHER_ORDERS[colour]
        return {low: everything, middle: place.step(middle, group), high: place.step(high, line)}

    def open_group(colour, group):
        right, left = pair(GATHER_ORDERS[colour][2])
        at = place_of(colour, group, 0)
        groups[colour][group] = (send(colour, at, full, right), send(colour, at, full, left))
        give(colour, at)

    def turn_group(colour, group):
        right, left = pair(GATHER_ORDERS[colour][2])
        to_right, to_left = groups[colour][group]
        to_right.wait_recv()
        on_right = send(colour, place_of(colour, group, 3), first, right)
        give(colour, place_of(colour, group, 3))
        to_left.wait_recv()
        on_left = send(colour, place_of(colour, group, 1), second, left)
        give(colour, place_of(colour, group, 1))
        ahead[colour][group] = (on_right, on_left)

    def close_group(colour, group):
        for copy in ahead[colour][group]:
            copy.wait_recv()
        give(colour, place_of(colour, group, 2))

    second_begun = []
    for colour in colours:
        for copy in passed[colour]:
            copy.wait_recv()
        low, middle, _ = GATHER_ORDERS[colour]
        right, left = pair(middle)
        at = {low: everything}
        second_begun.append(
            (
                send(colour, at, first, right),
                send(colour, at, second, left),
                send(colour, at, second, right),
                send(colour, at, first, left),
            )
        )
        open_group(colour, 0)
    hook(1)
    second_passed = []
    for colour in colours:
        low, middle, _ = GATHER_ORDERS[colour]
        right, left = pair(middle)
        near_right, near_left, rest_right, rest_left = second_begun[colour]
        near_right.wait_recv()
        on_right = send(colour, {low: everything, middle: place.step(middle, 3)}, first, right)
        near_left.wait_recv()
        on_left = send(colour, {low: everything, middle: place.step(middle, 1)}, second, left)
        second_passed.append((on_right, on_left))
    for colour in colours:
        second_begun[colour][2].wait_recv()
        open_group(colour, 3)
        second_begun[colour][3].wait_recv()
        open_group(colour, 1)
    for colour in colours:
        turn_group(colour, 0)
    hook(2)
    for colour in colours:
        for copy in second_passed[colour]:
            copy.wait_recv()
        open_group(colour, 2)
    for colour in colours:
        turn_group(colour, 3)
    for colour in colours:
        turn_group(colour, 1)
        close_group(colour, 0)
    hook(3)
    for colour in colours:
        turn_group(colour, 2)
        close_group(colour, 3)
        close_group(colour, 1)
    for colour in colours:
        close_group(colour, 2)
    for copy in handed:
        copy.wait_recv()


GATHER_COPIES = 3 * (4 + 6 + 16 + 16)


def sum_buffers(rows, width):
    shapes = []
    for lead in ((4, 4), (4,), ()):
        for size in (width // 2, width // 2, width, width):
            shapes.append(pltpu.VMEM((3, *lead, rows, size), jnp.bfloat16))
    return shapes


SUM_COPIES = 3 * 36


def exchange(place, copies, mine, theirs):
    given = {}
    for delta in (2, 1, 3, 0):
        lines = pl.ds(pl.multiple_of(place.step("z", delta) * 4 * TOK_DEV, TOK_DEV), 4 * TOK_DEV)
        given[delta] = copies.start(mine.at[lines, :], theirs.at[lines, :], place.sibling())
    return given


def torus_sum(place, copies, held, buffers, produce):
    width = held.shape[-1]
    first, second, full = pl.ds(0, width // 2), pl.ds(width // 2, width // 2), slice(None)
    colours = range(3)
    order_of_groups = (2, 1, 3, 0)

    def part(colour, at, features):
        where = [at[dim] if dim in at else place.at[dim] for dim in DIMS]
        return held.at[(*where, colour, slice(None), features)]

    def add(colour, at, spread_over, features, arrived):
        def one(at, pieces):
            target = part(colour, at, features)
            total = target[...].astype(jnp.float32)
            for piece in pieces:
                total = total + piece[...].astype(jnp.float32)
            target[...] = total.astype(jnp.bfloat16)

        if spread_over is None:
            one(at, arrived)
        else:

            def step(number, carry):
                one({**at, spread_over: number}, [piece.at[number] for piece in arrived])
                return carry

            lax.fori_loop(0, 4, step, 0)

    def lanes(ref, features):
        return ref if features is None else ref.at[(Ellipsis, features)]

    class Ring:
        def __init__(self, colour, dim, fixed, spread_over, refs):
            self.colour, self.dim, self.fixed, self.spread_over, self.refs = colour, dim, fixed, spread_over, refs
            self.right = place.device(**{dim: place.step(dim, 1)})
            self.left = place.device(**{dim: place.step(dim, 3)})

        def at(self, delta):
            return {**self.fixed, self.dim: place.step(self.dim, delta)}

        def send(self, delta, features, target, device):
            return copies.start(part(self.colour, self.at(delta), features), target, device)

        def far(self):
            self.far_right = self.send(2, first, self.refs[0], self.right)
            self.far_left = self.send(2, second, self.refs[1], self.left)

        def raw_right_part(self):
            self.raw_right = self.send(1, second, lanes(self.refs[2], second), self.right)

        def raw_left_part(self):
            self.raw_left = self.send(3, first, lanes(self.refs[3], first), self.left)

        def pass_right(self):
            self.far_right.wait_recv()
            add(self.colour, self.at(1), self.spread_over, first, [self.refs[0]])
            self.sum_right = self.send(1, first, lanes(self.refs[2], first), self.right)

        def pass_left(self):
            self.far_left.wait_recv()
            add(self.colour, self.at(3), self.spread_over, second, [self.refs[1]])
            self.sum_left = self.send(3, second, lanes(self.refs[3], second), self.left)

        def arrive(self):
            for copy in (self.raw_right, self.raw_left, self.sum_right, self.sum_left):
                copy.wait_recv()

        def close(self):
            self.arrive()
            add(self.colour, self.at(0), self.spread_over, full, [self.refs[2], self.refs[3]])

    rings, seconds, thirds = [], [], []
    for colour in colours:
        wide, middle, narrow = SUM_ORDERS[colour]
        by_group = []
        for number, group in enumerate(order_of_groups):
            refs = [ref.at[colour, number] for ref in buffers[0:4]]
            fixed = {middle: place.step(middle, group), narrow: slice(None)}
            by_group.append(Ring(colour, wide, fixed, narrow, refs))
        rings.append(by_group)
        refs = [ref.at[colour] for ref in buffers[4:8]]
        seconds.append(Ring(colour, middle, {narrow: slice(None)}, narrow, refs))
        thirds.append(Ring(colour, narrow, {}, None, [ref.at[colour] for ref in buffers[8:12]]))

    def open_ring(ring):
        ring.far()
        ring.raw_right_part()
        ring.raw_left_part()

    produce(2)
    for number in range(2):
        rings[2][number].far()
    produce(1)
    for number in range(2):
        rings[2][number].raw_right_part()
    produce(3)
    for number in range(2):
        rings[2][number].raw_left_part()
    produce(0)
    for number in range(2):
        for colour in range(2):
            open_ring(rings[colour][number])
    for number in range(4):
        for colour in colours:
            rings[colour][number].pass_right()
            rings[colour][number].pass_left()
        if number + 2 < 4:
            for colour in colours:
                open_ring(rings[colour][number + 2])
        for colour in colours:
            rings[colour][number].close()
            if number == 0:
                seconds[colour].far()
            elif number == 1:
                seconds[colour].raw_right_part()
            elif number == 2:
                seconds[colour].raw_left_part()
                seconds[colour].pass_right()
                seconds[colour].pass_left()
    for colour in colours:
        seconds[colour].close()
        open_ring(thirds[colour])
    for colour in colours:
        thirds[colour].pass_right()
        thirds[colour].pass_left()
    finals = []
    for colour in colours:
        thirds[colour].arrive()
        own = part(colour, {}, full)[...].astype(jnp.float32)
        last_left, last_right = thirds[colour].refs[2:4]
        finals.append(own + last_left[...].astype(jnp.float32) + last_right[...].astype(jnp.float32))
    return finals


def spread_kernel(
    tokens_ref, gain_ref, kv_ref, routes_attn_ref, routes_mlp_ref, wo_ref, wd_ref, wg_ref, wu_ref, router_ref,
    out, wkv_out, routes_out, wo_out, wd_out, both_out,
    rows, routes, opened, upward, both, send, recv, local,
):
    place = Place()
    fetches = [
        pltpu.make_async_copy(wg_ref, opened, local.at[3]),
        pltpu.make_async_copy(wu_ref, upward, local.at[4]),
    ]
    for fetch in fetches:
        fetch.start()
    copies = Copies(send, recv)
    t, e, c, y = place.t, place.e, place.c, place.at["y"]
    others = [{"tok": (t + delta) % 16, "exp": e} for delta in range(1, 16)]
    across = [{"tok": t, "exp": (e + delta) % 8} for delta in range(1, 8)]
    values = tokens_ref[y].astype(jnp.float32)
    scale = lax.rsqrt(jnp.mean(values * values, axis=-1, keepdims=True) + epsilon)
    rows[...] = (values * scale * gain_ref[...]).astype(jnp.bfloat16)
    half = pl.ds(pl.multiple_of(c * HALF, HALF), HALF)
    own = pltpu.make_async_copy(
        rows.at[:, :, half],
        out.at[place.at["z"], place.at["x"], y, :, :, half],
        local.at[0],
    )
    own.start()
    routes[...] = jnp.zeros_like(routes)
    routes[0:2, 0:TOK_DEV] = routes_attn_ref[...].astype(jnp.float32)
    routes[2:4, 0:TOK_DEV] = routes_mlp_ref[...].astype(jnp.float32)
    greet(others + across)
    own.wait()
    own_routes = pltpu.make_async_copy(routes, routes_out.at[t], local.at[1])
    own_routes.start()
    side = Copies(send.at[pl.ds(GATHER_COPIES, 24)], recv.at[pl.ds(GATHER_COPIES, 24)])
    sibling = place.sibling()
    source = t // 2
    hops = (y + 4 - t // 4) % 4
    columns = pl.ds(pl.multiple_of((t % 2) * 256, 256), 256)
    mine = pl.ds(pl.multiple_of(c * HALF, HALF), HALF)
    theirs = pl.ds(pl.multiple_of((1 - c) * HALF, HALF), HALF)
    rising = pl.ds(pl.multiple_of(c * HALF, QUARTER), QUARTER)
    falling = pl.ds(pl.multiple_of(c * HALF + QUARTER, QUARTER), QUARTER)
    right = place.device(y=(y + 1) % 4)
    left = place.device(y=(y + 3) % 4)
    is_source = e == source

    def fan(number, lines, device, fresh=False):
        at = GATHER_COPIES + 24 + number
        return pltpu.make_async_remote_copy(
            src_ref=kv_ref.at[lines, columns] if fresh else wkv_out.at[lines, :],
            dst_ref=wkv_out.at[lines, :],
            send_sem=send.at[at],
            recv_sem=recv.at[at],
            device_id=device,
            device_id_type=MESH,
        )

    keep = pltpu.make_async_copy(kv_ref.at[mine, columns], wkv_out.at[mine, :], local.at[2])

    def first_hop():
        @pl.when(is_source)
        def _():
            fan(0, theirs, sibling, True).start()
            fan(1, rising, right, True).start()
            fan(2, falling, left, True).start()
            keep.start()

        for device in others:
            routed.append(side.start(routes, routes_out.at[t], device))
        routed.append(side.start(wo_ref.at[:, theirs], wo_out, sibling))
        for number in range(4):
            lanes = pl.ds(pl.multiple_of(number * 512 + (1 - c) * 256, 256), 256)
            target = wd_out.at[:, pl.ds(number * 256, 256)]
            routed.append(side.start(wd_ref.at[:, lanes], target, sibling))

    def second_hop():
        @pl.when((hops == 0) & jnp.logical_not(is_source))
        def _():
            fan(0, mine, sibling).wait_recv()
            fan(1, rising, right).start()
            fan(2, falling, left).start()

        @pl.when(hops == 1)
        def _():
            fan(1, rising, right).wait_recv()
            fan(1, rising, right).start()

        @pl.when(hops == 3)
        def _():
            fan(2, falling, left).wait_recv()
            fan(2, falling, left).start()

    def third_hop():
        @pl.when(hops == 2)
        def _():
            fan(1, rising, right).wait_recv()
            fan(1, rising, right).start()
            fan(2, falling, left).wait_recv()
            fan(2, falling, left).start()

    def last_hop():
        @pl.when(hops == 1)
        def _():
            fan(2, falling, left).wait_recv()

        @pl.when(hops == 3)
        def _():
            fan(1, rising, right).wait_recv()

        @pl.when(is_source)
        def _():
            keep.wait()

        shared.append(side.start(wkv_out.at[mine, :], wkv_out.at[mine, :], sibling))

    def turned(ref, shift, width):
        eye = jnp.where(
            lax.broadcasted_iota(jnp.int32, (ref.shape[0], width), 0) + shift
            == lax.broadcasted_iota(jnp.int32, (ref.shape[0], width), 1),
            1.0,
            0.0,
        ).astype(jnp.bfloat16)

        def some(at):
            return lax.dot_general(
                ref[:, at], eye, (((0,), (0,)), ((), ())), preferred_element_type=jnp.float32
            ).astype(jnp.bfloat16)

        return some

    def turn_gate():
        fetches[0].wait()
        some = turned(opened, 0, BLK)
        for number in range(4):
            at = slice(number * 512, (number + 1) * 512)
            both[at, 0:BLK] = some(at)

    def turn_up():
        fetches[1].wait()
        some = turned(upward, 0, BLK)
        routing = turned(router_ref, FF_DEV - 2 * HD, HD)
        for number in range(4):
            at = slice(number * 512, (number + 1) * 512)
            both[at, BLK : 2 * BLK] = some(at)
            both[at, BLK + 2 * HD : 2 * BLK] += routing(at)
        stored.start()

    stored = pltpu.make_async_copy(both, both_out, local.at[5])

    def second_step():
        second_hop()
        turn_gate()

    def third_step():
        third_hop()
        turn_up()

    routed, shared = [], []
    torus_gather(place, copies, out, (first_hop, second_step, third_step, last_hop))
    stored.wait()
    shared[0].wait_recv()
    own_routes.wait()
    for copy in routed:
        copy.wait_recv()

    @pl.when(is_source)
    def _():
        fan(0, theirs, sibling, True).wait_send()

    @pl.when(hops != 3)
    def _():
        fan(1, rising, right).wait_send()

    @pl.when(hops != 1)
    def _():
        fan(2, falling, left).wait_send()

    copies.drain()
    side.drain()


def route_columns(routes_ref):
    eye = jnp.where(
        lax.broadcasted_iota(jnp.int32, (8, HD), 0) == lax.broadcasted_iota(jnp.int32, (8, HD), 1), 1.0, 0.0
    )
    parts = [
        lax.dot_general(
            routes_ref[number][:, :TOK_DEV], eye, (((0,), (0,)), ((), ())), preferred_element_type=jnp.float32
        )
        for number in range(2)
    ]
    return jnp.concatenate(parts, axis=0)


def pair_gate(first, second, expert, logits, base):
    chosen = (first == expert) | (second == expert)
    other = first + second - expert
    lane = lax.broadcasted_iota(jnp.int32, logits.shape, 1).astype(jnp.float32) - base
    own_logit = jnp.sum(jnp.where(lane == expert, logits, 0.0), axis=1, keepdims=True)
    other_logit = jnp.sum(jnp.where(lane == other, logits, 0.0), axis=1, keepdims=True)
    return chosen, jnp.where(chosen, 1.0 / (1.0 + jnp.exp(other_logit - own_logit)), 0.0)


PAGE_ROWS = PAGE + 16


def attend_kernel(
    lengths, table, x_ref, h1_ref, wq_ref, wkv_ref, router_ref, kv_ref, frequency_ref, routes_ref,
    out_ref, pages_ref,
    keys, values, weights, inner_cos, inner_sin, page_rows, page_sems,
):
    block = pl.program_id(0)
    tok = lax.axis_index("tok")
    expert = lax.axis_index("exp").astype(jnp.float32)
    second_start = lengths[0]
    third_start = lengths[0] + lengths[1]
    frequency = jnp.broadcast_to(frequency_ref[...], (8, HD))
    sign = jnp.where(lax.broadcasted_iota(jnp.int32, (1, HD), 1) < 64, -1.0, 1.0)

    def find(slot):
        def look(number, carry):
            begin, count, start = carry
            prompt, page = number // table.shape[2], number % table.shape[2]
            its_start = jnp.where(prompt == 0, 0, jnp.where(prompt == 1, second_start, third_start))
            remaining = lengths[prompt] - page * PAGE
            hit = (table[prompt, 0, page] == tok) & (table[prompt, 1, page] == slot) & (remaining > 0)
            return (
                jnp.where(hit, its_start + page * PAGE, begin),
                jnp.where(hit, jnp.minimum(remaining, PAGE), count),
                jnp.where(hit, its_start, start),
            )

        zero = jnp.int32(0)
        begin, count, start = lax.fori_loop(0, table.shape[0] * table.shape[2], look, (zero, zero, zero))
        aligned = jnp.minimum(begin // 16 * 16, TOKENS - PAGE_ROWS)
        return begin, count, start, pl.multiple_of(aligned, 16)

    def page_copy(slot, aligned):
        return pltpu.make_async_copy(
            h1_ref.at[pl.ds(aligned, PAGE_ROWS), :], page_rows.at[slot], page_sems.at[slot]
        )

    @pl.when(block == 0)
    def _():
        for slot in range(2):
            page_copy(slot, find(slot)[3]).start()
        weights[:, 0:HD] = wq_ref[...]
        weights[:, HD : 3 * HD] = wkv_ref[...]
        eye = jnp.where(
            lax.broadcasted_iota(jnp.int32, (8, HD), 0) == lax.broadcasted_iota(jnp.int32, (8, HD), 1), 1.0, 0.0
        )
        weights[:, 3 * HD :] = lax.dot_general(
            router_ref[...].astype(jnp.float32), eye, (((0,), (0,)), ((), ())), preferred_element_type=jnp.float32
        ).astype(jnp.bfloat16)
        angle = lax.broadcasted_iota(jnp.int32, (BLK, HD), 0).astype(jnp.float32) * frequency_ref[...]
        inner_cos[...] = jnp.cos(angle)
        inner_sin[...] = jnp.sin(angle)

    def outer(offset):
        angle = frequency * offset.astype(jnp.float32)
        return jnp.cos(angle)[0:1], jnp.sin(angle)[0:1]

    def turn(base_cos, base_sin, in_cos, in_sin):
        return base_cos * in_cos - base_sin * in_sin, (base_sin * in_cos + base_cos * in_sin) * sign

    row = lax.broadcasted_iota(jnp.int32, (BLK, 1), 0) + block * BLK
    in_second, in_third = row >= second_start, row >= third_start
    start = jnp.where(in_third, third_start, jnp.where(in_second, second_start, 0))
    bases = [outer(block * BLK - begin) for begin in (jnp.int32(0), second_start, third_start)]
    base_cos, base_sin = (
        jnp.where(in_third, bases[2][number], jnp.where(in_second, bases[1][number], bases[0][number]))
        for number in range(2)
    )
    cosine, sine = turn(base_cos, base_sin, inner_cos[...], inner_sin[...])

    def rotate(v):
        return (v * cosine + pltpu.roll(v, 64, 1) * sine).astype(jnp.bfloat16)

    projected = jnp.dot(x_ref[...], weights[...], preferred_element_type=jnp.float32)
    here = pl.ds(pl.multiple_of(block * BLK, BLK), BLK)
    keys[here, :] = rotate(projected[:, HD : 2 * HD])
    values[here, :] = projected[:, 2 * HD : 3 * HD].astype(jnp.bfloat16)
    queries = rotate(projected[:, :HD])
    columns = route_columns(routes_ref)
    chosen, gate = pair_gate(columns[:, 0:1], columns[:, 1:2], expert, projected[:, 3 * HD :], 0.0)
    row_number = lax.broadcasted_iota(jnp.int32, (BLK, BLK), 0)
    column_number = lax.broadcasted_iota(jnp.int32, (BLK, BLK), 1)
    below = jnp.where(row_number >= column_number, 1.0, 0.0).astype(jnp.bfloat16)
    flags = jnp.broadcast_to(jnp.where(chosen, 1.0, 0.0), (BLK, HD)).astype(jnp.bfloat16)
    rank = jnp.dot(below, flags, preferred_element_type=jnp.float32)[:, 0:1] - 1.0
    slot_number = lax.broadcasted_iota(jnp.int32, (BLK, SLOTS_BLK), 1).astype(jnp.float32)
    placing = jnp.where(chosen & (rank == slot_number), 1.0, 0.0).astype(jnp.bfloat16)
    lane = lax.broadcasted_iota(jnp.int32, (BLK, HD), 1)
    inside = lax.broadcasted_iota(jnp.int32, (BLK, HD), 0)
    digits = jnp.where(
        lane == 0,
        inside >> 4,
        jnp.where(lane == 1, inside & 15, jnp.where(lane == 2, start >> 6, jnp.where(lane == 3, start & 63, 0))),
    ).astype(jnp.float32).astype(jnp.bfloat16)
    taken = lax.dot_general(
        placing,
        jnp.concatenate([queries, digits], axis=1),
        (((0,), (0,)), ((), ())),
        preferred_element_type=jnp.float32,
    )
    picked = taken[:, :HD].astype(jnp.bfloat16)
    told = taken[:, HD:]
    highest_key = told[:, 0:1] * 16.0 + told[:, 1:2] + (block * BLK).astype(jnp.float32)
    lowest_key = told[:, 2:3] * 64.0 + told[:, 3:4]
    key_lane = lax.broadcasted_iota(jnp.int32, (SLOTS_BLK, BLK), 1)

    def visit(tile, carry):
        highest, denominator, summed = carry
        there = pl.ds(pl.multiple_of(tile * BLK, BLK), BLK)
        scores = lax.dot_general(
            picked, keys[there, :], (((1,), (1,)), ((), ())), preferred_element_type=jnp.float32
        ) * (HD**-0.5)
        number = (key_lane + tile * BLK).astype(jnp.float32)
        scores = jnp.where((number >= lowest_key) & (number <= highest_key), scores, -1e30)
        newest = jnp.maximum(highest, jnp.max(scores, axis=1, keepdims=True))
        shares = jnp.exp(scores - newest)
        shrink = jnp.exp(highest - newest)
        denominator = denominator * shrink + jnp.sum(shares, axis=1, keepdims=True)
        summed = summed * shrink + jnp.dot(
            shares.astype(jnp.bfloat16), values[there, :], preferred_element_type=jnp.float32
        )
        return newest, denominator, summed

    begin = block * BLK
    begin_of = jnp.where(begin >= third_start, third_start, jnp.where(begin >= second_start, second_start, 0))
    _, denominator, summed = lax.fori_loop(
        begin_of // BLK,
        block + 1,
        visit,
        (
            jnp.full((SLOTS_BLK, 1), -1e30, jnp.float32),
            jnp.zeros((SLOTS_BLK, 1), jnp.float32),
            jnp.zeros((SLOTS_BLK, HD), jnp.float32),
        ),
    )
    attended = (summed / denominator).astype(jnp.bfloat16)
    dense = jnp.dot(placing, attended, preferred_element_type=jnp.float32)
    out_ref[...] = (dense * gate).astype(jnp.bfloat16)

    @pl.when(block == pl.num_programs(0) - 1)
    def _():
        for slot in range(2):
            begin, count, start, aligned = find(slot)
            page_copy(slot, aligned).wait()
            part = jnp.dot(page_rows[slot], kv_ref[...], preferred_element_type=jnp.float32)
            page_cos, page_sin = turn(*outer(aligned - start), inner_cos[0:PAGE_ROWS], inner_sin[0:PAGE_ROWS])
            pieces = []
            for head in range(2):
                key = part[:, head * 256 : head * 256 + HD]
                pieces.append(key * page_cos + pltpu.roll(key, 64, 1) * page_sin)
                pieces.append(part[:, head * 256 + HD : (head + 1) * 256])
            run = jnp.concatenate(pieces, axis=1).astype(jnp.bfloat16)
            to = lax.broadcasted_iota(jnp.int32, (PAGE, PAGE_ROWS), 0)
            source = lax.broadcasted_iota(jnp.int32, (PAGE, PAGE_ROWS), 1)
            moving = jnp.where((source == to + (begin - aligned)) & (to < count), 1.0, 0.0).astype(jnp.bfloat16)
            pages_ref[slot] = jnp.dot(moving, run, preferred_element_type=jnp.float32).astype(jnp.bfloat16)


def middle_kernel(
    heads_ref, wo_ref, wo_pair_ref, tokens_ref, gain_ref,
    out, residual_out,
    paired, weights, held, shared, squares, rows, residual, send, recv, local, *buffers,
):
    place = Place()
    t, e, c, y = place.t, place.e, place.c, place.at["y"]
    across = [{"tok": t, "exp": (e + delta) % 8} for delta in range(1, 8)]
    around = [device for number, device in enumerate(place.neighbours()) if number in (1, 2, 3, 4)]
    greet(around + across)
    copies = Copies(send, recv)
    sibling = place.sibling()
    half = pl.ds(pl.multiple_of(c * HALF, HALF), HALF)
    given = exchange(place, copies, heads_ref, paired)
    weights[0:HD, :] = wo_ref[:, half]
    weights[HD : 2 * HD, :] = wo_pair_ref[...]

    def produce(delta):
        given[delta].wait_recv()
        z = place.step("z", delta)

        def project(x, carry):
            lines = pl.ds(pl.multiple_of((z * 4 + x) * TOK_DEV, TOK_DEV), TOK_DEV)
            both = jnp.concatenate([heads_ref[lines, :], paired[lines, :]], axis=1)
            part = jnp.dot(both, weights[...], preferred_element_type=jnp.float32)
            held[z, x] = part.astype(jnp.bfloat16).reshape(4, 3, 16, HALF)
            return carry

        lax.fori_loop(0, 4, project, 0)

    sums = torus_sum(place, copies, held, buffers, produce)
    square = []
    for colour in range(3):
        value = tokens_ref[y, colour, :, half].astype(jnp.float32) + sums[colour]
        residual[colour] = value
        square.append(jnp.sum(value * value, axis=-1, keepdims=True))
        shared[colour] = jnp.broadcast_to(square[colour], (16, HD))
    swapped = copies.start(shared, squares, sibling)
    for colour in range(3):
        for number in range(4):
            rows_here = pl.ds(colour * 16, 16)
            residual_out_part = residual[colour, :, number * 256 : (number + 1) * 256]
            buffers[-1][number, rows_here, :] = residual_out_part
    pieces = buffers[-1]
    base = send.shape[0] - 4

    def piece(number, sender):
        return pltpu.make_async_remote_copy(
            src_ref=pieces.at[number],
            dst_ref=residual_out.at[sender],
            send_sem=send.at[base + number],
            recv_sem=recv.at[base + sender],
            device_id={"tok": t, "exp": 4 * c + number},
            device_id_type=MESH,
        )

    for number in range(4):

        @pl.when(4 * c + number == e)
        def _():
            keep = pltpu.make_async_copy(pieces.at[number], residual_out.at[y], local.at[1])
            keep.start()
            keep.wait()

        @pl.when(4 * c + number != e)
        def _():
            piece(number, y).start()

    swapped.wait_recv()
    for colour in range(3):
        total = square[colour] + squares[colour][:, 0:1]
        scale = lax.rsqrt(total * (1.0 / D) + epsilon)
        rows[colour] = (residual[colour] * scale * gain_ref[:, half]).astype(jnp.bfloat16)
    own = pltpu.make_async_copy(
        rows, out.at[place.at["z"], place.at["x"], y, :, :, half], local.at[0]
    )
    own.start()
    own.wait()
    torus_gather(place, copies, out)
    for sender in range(4):
        itself = (y == sender) & (c == e // 4)

        @pl.when(jnp.logical_not(itself))
        def _():
            piece(0, sender).wait_recv()

    for number in range(4):

        @pl.when(4 * c + number != e)
        def _():
            piece(number, y).wait_send()

    copies.drain()


def hidden_kernel(x_ref, weights_ref, routes_ref, out_ref):
    expert = lax.axis_index("exp").astype(jnp.float32)
    both = jnp.dot(x_ref[...], weights_ref[...], preferred_element_type=jnp.float32)
    columns = route_columns(routes_ref)
    _, gate = pair_gate(columns[:, 2:3], columns[:, 3:4], expert, both[:, 5 * HD :], float(FF_DEV - 2 * HD))
    opened, upward = both[:, :FF_DEV], both[:, BLK : BLK + FF_DEV]
    hidden = opened / (1.0 + jnp.exp(-opened)) * upward
    out_ref[...] = (hidden * gate).astype(jnp.bfloat16)


def last_kernel(
    hidden_ref, wd_ref, wd_pair_ref, residual_ref,
    out_ref,
    paired, held, send, recv, *buffers,
):
    place = Place()
    c = place.c
    greet(place.neighbours())
    copies = Copies(send, recv)
    given = exchange(place, copies, hidden_ref, paired)

    def produce(delta):
        given[delta].wait_recv()
        z = place.step("z", delta)

        def project(x, carry):
            lines = pl.ds(pl.multiple_of((z * 4 + x) * TOK_DEV, TOK_DEV), TOK_DEV)
            own, pair = hidden_ref[lines, :], paired[lines, :]
            for at in range(4):
                lanes = pl.ds(pl.multiple_of(at * 512 + c * 256, 256), 256)
                part = jnp.dot(own, wd_ref[:, lanes], preferred_element_type=jnp.float32)
                part += jnp.dot(
                    pair, wd_pair_ref[:, at * 256 : (at + 1) * 256], preferred_element_type=jnp.float32
                )
                held[z, x, at] = part.astype(jnp.bfloat16).reshape(3, 64, 256)
            return carry

        lax.fori_loop(0, 4, project, 0)

    sums = torus_sum(place, copies, held, buffers, produce)
    for colour in range(3):
        lines = slice(colour * 64, (colour + 1) * 64)
        out_ref[lines, :] = (residual_ref[lines, :] + sums[colour]).astype(jnp.bfloat16)
    copies.drain()


def shards(
    tokens,
    gain_attn,
    router_attn,
    kv_weight,
    query_weight,
    out_weight,
    gain_mlp,
    router_mlp,
    gate_weight,
    up_weight,
    down_weight,
    routes_attn,
    routes_mlp,
    lengths,
    page_table,
):
    bf16 = jnp.bfloat16
    struct = jax.ShapeDtypeStruct
    tokens_parts = tokens.reshape(4, 3, 16, D)
    spread_count = GATHER_COPIES + 24 + 3
    gathered, wkv, routes, wo_pair, wd_pair, both = pl.pallas_call(
        spread_kernel,
        out_shape=(
            struct((4, 4, 4, 3, 16, D), bf16),
            struct((D, 256), bf16),
            struct((16, 8, 256), jnp.float32),
            struct((HD, HALF), bf16),
            struct((FF_DEV, HALF), bf16),
            struct((D, 2 * BLK), bf16),
        ),
        in_specs=[VMEM, VMEM, ANY, VMEM, VMEM, ANY, ANY, ANY, ANY, VMEM],
        out_specs=(ANY,) * 6,
        scratch_shapes=[
            pltpu.VMEM((3, 16, D), bf16),
            pltpu.VMEM((8, 256), jnp.float32),
            pltpu.VMEM((FF_DEV, D), bf16),
            pltpu.VMEM((FF_DEV, D), bf16),
            pltpu.VMEM((D, 2 * BLK), bf16),
            pltpu.SemaphoreType.DMA((spread_count,)),
            pltpu.SemaphoreType.DMA((spread_count,)),
            pltpu.SemaphoreType.DMA((6,)),
        ],
        compiler_params=pltpu.CompilerParams(collective_id=0, has_side_effects=True),
        name="spread",
    )(
        tokens_parts, gain_attn.reshape(1, 1, D), kv_weight, routes_attn.T, routes_mlp.T, out_weight[0], down_weight[0],
        gate_weight[0].T, up_weight[0].T, router_mlp.T,
    )
    h1 = gathered.reshape(TOKENS, D)
    frequency = (10000.0 ** -(np.arange(HD) % 64 * (2.0 / HD))).astype(np.float32).reshape(1, HD)
    steps = TOKENS // BLK

    def whole(*shape):
        return pl.BlockSpec(shape, lambda i, *_: (0,) * len(shape))

    def lines(width):
        return pl.BlockSpec((BLK, width), lambda i, *_: (i, 0))

    routes_spec = pl.BlockSpec((2, 8, 256), lambda i, *_: (i, 0, 0))
    heads, kv_pages = pl.pallas_call(
        attend_kernel,
        out_shape=(struct((TOKENS, HD), bf16), struct((2, PAGE, 512), bf16)),
        grid_spec=pltpu.PrefetchScalarGridSpec(
            num_scalar_prefetch=2,
            grid=(steps,),
            in_specs=[
                lines(D), ANY, whole(D, HD), whole(D, 256), whole(8, D), whole(D, 512), whole(1, HD), routes_spec,
            ],
            out_specs=(lines(HD), whole(2, PAGE, 512)),
            scratch_shapes=[
                pltpu.VMEM((TOKENS, HD), bf16),
                pltpu.VMEM((TOKENS, HD), bf16),
                pltpu.VMEM((D, 4 * HD), bf16),
                pltpu.VMEM((BLK, HD), jnp.float32),
                pltpu.VMEM((BLK, HD), jnp.float32),
                pltpu.VMEM((2, PAGE_ROWS, D), bf16),
                pltpu.SemaphoreType.DMA((2,)),
            ],
        ),
        name="attend",
    )(lengths, jnp.swapaxes(page_table, 1, 2), h1, h1, query_weight[0], wkv, router_attn.T, kv_weight, jnp.asarray(frequency), routes)

    middle_count = 5 + SUM_COPIES + GATHER_COPIES + 4
    gathered, residual = pl.pallas_call(
        middle_kernel,
        out_shape=(struct((4, 4, 4, 3, 16, D), bf16), struct((4, 48, 256), jnp.float32)),
        in_specs=[VMEM] * 5,
        out_specs=(ANY, ANY),
        scratch_shapes=[
            pltpu.VMEM((TOKENS, HD), bf16),
            pltpu.VMEM((2 * HD, HALF), bf16),
            pltpu.VMEM((4, 4, 4, 3, 16, HALF), bf16),
            pltpu.VMEM((3, 16, HD), jnp.float32),
            pltpu.VMEM((3, 16, HD), jnp.float32),
            pltpu.VMEM((3, 16, HALF), bf16),
            pltpu.VMEM((3, 16, HALF), jnp.float32),
            pltpu.SemaphoreType.DMA((middle_count,)),
            pltpu.SemaphoreType.DMA((middle_count,)),
            pltpu.SemaphoreType.DMA((2,)),
            *sum_buffers(16, HALF),
            pltpu.VMEM((4, 48, 256), jnp.float32),
        ],
        compiler_params=pltpu.CompilerParams(collective_id=1, has_side_effects=True),
        name="middle",
    )(heads, out_weight[0], wo_pair, tokens_parts, gain_mlp.reshape(1, D))
    h2 = gathered.reshape(TOKENS, D)

    hidden = pl.pallas_call(
        hidden_kernel,
        out_shape=struct((TOKENS, FF_DEV), bf16),
        grid_spec=pltpu.PrefetchScalarGridSpec(
            num_scalar_prefetch=0,
            grid=(steps,),
            in_specs=[lines(D), whole(D, 2 * BLK), routes_spec],
            out_specs=lines(FF_DEV),
        ),
        name="hidden",
    )(h2, both, routes)

    last_count = 4 + SUM_COPIES
    mixed = pl.pallas_call(
        last_kernel,
        out_shape=struct((TOK_DEV, 256), bf16),
        in_specs=[VMEM] * 4,
        out_specs=VMEM,
        scratch_shapes=[
            pltpu.VMEM((TOKENS, FF_DEV), bf16),
            pltpu.VMEM((4, 4, 4, 3, 64, 256), bf16),
            pltpu.SemaphoreType.DMA((last_count,)),
            pltpu.SemaphoreType.DMA((last_count,)),
            *sum_buffers(64, 256),
        ],
        compiler_params=pltpu.CompilerParams(collective_id=2, has_side_effects=True),
        name="last",
    )(hidden, down_weight[0], wd_pair, residual.reshape(TOK_DEV, 256))
    return (mixed, kv_pages)


def solution(mesh):
    return jax.shard_map(
        shards,
        mesh=mesh,
        in_specs=(
            P("tok", None),
            P(),
            P(),
            P(None, "exp"),
            P("exp", None, "tok"),
            P("exp", "tok", None),
            P(),
            P(),
            P("exp", None, "tok"),
            P("exp", None, "tok"),
            P("exp", "tok", None),
            P("tok", None),
            P("tok", None),
            P(),
            P(),
        ),
        out_specs=(P("tok", "exp"), P("tok", None, "exp")),
        check_vma=False,
    )
```
